256 devices in a mesh: band: 16 (over y, x_lo, core), cols: 16 (over x_hi, z).
Axes of the slice: x: 4 (x_hi: 2, x_lo: 2; x = x_hi * 2 + x_lo), y: 4, z: 8, core: 2. Of those that a mesh axis runs over, the one named last changes fastest.
Arguments:
- band_diagonals: float32 [256, 6144], P('cols', 'band'), may hold values from -0.4 to 0.4, as said below
- eigenvectors: float32 [6144, 2048], P('band', 'cols'), may hold values from -4 to 4
Outputs:
- band_result: float32 [256, 6144], P('cols', 'band')
- transformed: float32 [6144, 2048], P('band', 'cols')
The draws below stay inside these ranges and needn't reach their ends.
Inputs may be any that keep to these rules, and one draw needn't show every extreme that they name: `band_diagonals`: entry [k, r] is the matrix's entry in row r and column r - k; it is zero where k > 128 or r < k.
All inputs are finite; a program needn't handle non-finite values.
Results may differ from the reference program's by a relative error of at most 0.0003.
Values sent between devices are 32-bit elements; how exact they have to be, the bound alone decides.
No kernel may reach another device: no remote copies, remote signals or barrier semaphores. Data moves between devices by JAX's collectives and lax.ppermute only.
A program may use at most 64 MiB of HBM per device.

```python
import jax
import jax.numpy as jnp
from jax import lax

BW = 128
SWEEPS = 4
ORDER = 6144
EIGVECS = 2048


def draw_band_diagonals(key, part):
    rough = jnp.clip(jax.random.normal(key, (2 * BW, ORDER), jnp.float32), -4.0, 4.0) * 0.1
    diag_index = lax.broadcasted_iota(jnp.int32, (2 * BW, ORDER), 0)
    row_index = lax.broadcasted_iota(jnp.int32, (2 * BW, ORDER), 1)
    keep = (diag_index <= BW) & (row_index >= diag_index)
    return jnp.where(keep, rough, 0.0)


def levels(stream_key, shape, pieces, least, high):
    loudness, own = 1.0, jax.random.fold_in(stream_key, 6)
    for position, blocks in pieces:
        steps = jnp.exp(jax.random.uniform(jax.random.fold_in(own, position), (blocks,), jnp.float32, least / len(pieces), high / len(pieces)))
        loudness = loudness * jnp.repeat(steps, shape[position] // blocks).reshape([-1 if axis == position else 1 for axis in range(len(shape))])
    return loudness


def noise(stream_key, extent, spread, bound, cuts=(), kind=jnp.bfloat16):
    drawn = jax.random.normal(stream_key, extent, jnp.float32) * spread
    if len(cuts) > 0:
        drawn = levels(stream_key, extent, cuts, -0.22, 0.18) * drawn
    return jnp.clip(drawn, min=-bound, max=bound).astype(kind)


def setup_inputs(seed: int = 0) -> dict:
    key_list = jax.random.split(jax.random.key(seed), 3)
    band_diagonals = draw_band_diagonals(jax.random.fold_in(key_list[2], 71), 0)
    eigenvectors = noise(key_list[1], (ORDER, EIGVECS), 1.0, 4.0, ((0, 16), (1, 16)), jnp.float32)
    return {"band_diagonals": band_diagonals, "eigenvectors": eigenvectors}


HIGHEST = lax.Precision.HIGHEST

def skew_rows(block_rows):
    row_count, col_count = block_rows.shape
    flipped = block_rows[:, ::-1]
    padded = jnp.pad(flipped, ((0, 0), (0, row_count)))
    flat_cells = padded.reshape(-1)[:row_count * (col_count + row_count - 1)]
    return flat_cells.reshape(row_count, col_count + row_count - 1)

def unskew_rows(dense_rows, col_count):
    row_count = dense_rows.shape[0]
    flat_cells = jnp.pad(dense_rows.reshape(-1), (0, row_count))
    grid_cells = flat_cells.reshape(row_count, col_count + row_count)
    return grid_cells[:, :col_count][:, ::-1]

def chase_step(region, first_step):
    double = region.shape[0]
    half_width = double // 2
    dense_rows = skew_rows(region)
    offset = half_width - 1
    upper_rows = dense_rows[:half_width, offset:offset + double]
    lower_rows = dense_rows[half_width:, offset + half_width:offset + double]
    left_part = upper_rows[:, :half_width]
    window = upper_rows[:, half_width:]
    column = jnp.where(first_step, left_part[:, half_width - 1], left_part[:, 0])
    length = jnp.sqrt(jnp.sum(column * column))
    vector = column.at[0].add(length)
    factor = 2.0 / jnp.sum(vector * vector)
    mirror = window + window.T - jnp.diag(jnp.diag(window))
    across = factor * jnp.dot(vector, left_part, precision=HIGHEST)
    inside = factor * jnp.dot(mirror, vector, precision=HIGHEST)
    beneath = factor * jnp.dot(lower_rows, vector, precision=HIGHEST)
    inside = inside - 0.5 * factor * jnp.dot(vector, inside, precision=HIGHEST) * vector
    left_part = left_part - vector[:, None] * across[None, :]
    window = window - jnp.tril(vector[:, None] * inside[None, :] + inside[:, None] * vector[None, :])
    lower_rows = lower_rows - beneath[:, None] * vector[None, :]
    cleared = jnp.zeros_like(column).at[0].set(-length)
    left_part = jnp.where(first_step, left_part.at[:, half_width - 1].set(cleared), left_part.at[:, 0].set(cleared))
    dense_rows = dense_rows.at[:half_width, offset:offset + double].set(jnp.concatenate([left_part, window], 1))
    dense_rows = dense_rows.at[half_width:, offset + half_width:offset + double].set(lower_rows)
    return (unskew_rows(dense_rows, double), vector, factor)

def reference(band_diagonals, eigenvectors):
    band_rows = band_diagonals.T
    step_count = ORDER // BW - 2
    kept_vectors = []
    kept_factors = []
    for sweep_number in range(SWEEPS):

        def advance(carry, step_index):
            anchor = (sweep_number + 1 + step_index * BW).astype(jnp.int32)
            region = lax.dynamic_slice_in_dim(carry, anchor, 2 * BW, 0)
            region, vector, factor = chase_step(region, step_index == 0)
            carry = lax.dynamic_update_slice_in_dim(carry, region, anchor, 0)
            return (carry, (vector, factor))
        band_rows, (sweep_vectors, sweep_factors) = lax.scan(advance, band_rows, jnp.arange(step_count, dtype=jnp.int32))
        kept_vectors.append(sweep_vectors)
        kept_factors.append(sweep_factors)
    result = eigenvectors
    for sweep_number in reversed(range(SWEEPS)):
        lead_rows = sweep_number + 1
        sweep_vectors = kept_vectors[sweep_number]
        sweep_factors = kept_factors[sweep_number]
        blocks = result[lead_rows:lead_rows + step_count * BW].reshape(step_count, BW, EIGVECS)
        inner_sums = jnp.einsum('kb,kbc->kc', sweep_vectors, blocks, precision=HIGHEST)
        blocks = blocks - (sweep_factors[:, None] * sweep_vectors)[:, :, None] * inner_sums[:, None, :]
        result = result.at[lead_rows:lead_rows + step_count * BW].set(blocks.reshape(step_count * BW, EIGVECS))
    return (band_rows.T, result)
```

```python
import jax
import jax.numpy as jnp
from jax import lax
from jax.experimental import pallas as pl
from jax.experimental.pallas import tpu as pltpu
from jax.sharding import PartitionSpec as P

SWEEPS = 4
BW = 128
OFF = 255
HALO = 512
TAIL = 8
SLOTS = 8


def lane_sum(x):
    return jnp.sum(x, axis=1, keepdims=True)


def row_sum(x):
    return jnp.sum(x, axis=0, keepdims=True)


def spread(x):
    return jnp.broadcast_to(x, (x.shape[0], BW))


def chase_kernel(place, reversed_diags, last_diag, slab, band_out, slab_out, *scratch):
    lefts = scratch[0:5]
    diags = scratch[5:10]
    kept, beneath, rows, work = scratch[10:14]
    order = reversed_diags.shape[1]
    steps = order // BW - 2
    device, slice_index = place[0], place[1]
    first_window = (device * slab_out.shape[0]) // BW - HALO // BW

    lane = lax.broadcasted_iota(jnp.int32, (BW, BW), 1)
    sub = lax.broadcasted_iota(jnp.int32, (BW, BW), 0)
    line = lax.broadcasted_iota(jnp.int32, (1, BW), 1)
    turn = (lane - sub) & (BW - 1)

    zero_block = jnp.zeros((BW, BW), jnp.float32)
    for ref in lefts + diags:
        for block in range(4):
            ref[pl.ds(block * BW, BW), :] = zero_block
    for ref in (lefts[0], diags[0]):
        start = (order + OFF) // 8 * 8
        ref[pl.ds(start, ref.shape[0] - start), :] = jnp.zeros((ref.shape[0] - start, BW), jnp.float32)
    for s in range(SWEEPS):
        beneath[s] = zero_block
        rows[s] = jnp.zeros((8, BW), jnp.float32)
        for slot in range(SLOTS):
            kept[s, slot] = zero_block

    own = (sub - 1) & (BW - 1)

    def lay_out(block, carry):
        begin = pl.multiple_of(block * BW, BW)
        tile = reversed_diags[:, pl.ds(begin, BW)].T
        tile = pltpu.roll(tile, 0, 1, stride=1, stride_axis=0)
        far = pltpu.roll(spread_rows(last_diag[:, pl.ds(begin, BW)]), BW - 1, 1)
        left = jnp.where(lane > own, tile, jnp.where(lane == own, far, 0.0))
        lefts[0][pl.ds(begin + OFF, BW), :] = left
        diags[0][pl.ds(begin + OFF, BW), :] = jnp.where(lane <= own, tile, 0.0)
        return carry

    def spread_rows(x):
        return jnp.broadcast_to(x[0:1, :], (BW, BW))

    lax.fori_loop(0, order // BW, lay_out, 0)

    def mirror(block, carry):
        at = pl.ds(pl.multiple_of(block * BW, 8), BW)
        lower = diags[0][at, :]
        diags[0][at, :] = jnp.where(lane <= sub, lower, lower.T)
        return carry

    lax.fori_loop(1, order // BW + 2, mirror, 0)

    def slot_of(window):
        index = window - first_window
        return jnp.where((index >= 0) & (index < SLOTS - 1), index, SLOTS - 1)

    def left_over(s, last):
        entries = jnp.zeros((1, BW), jnp.float32)
        for back in range(1, s + 1):
            entry = work[s - back, back : back + 1, :]
            entries = jnp.where((line == s - back) & last, entry, entries)
        return entries

    def stage(t, carry):
        for s in reversed(range(SWEEPS)):
            k = jnp.maximum(t - 2 * s, -1)
            following = t - 2 * s + 1
            base = k * BW + (s + 1 + OFF)
            here = pl.ds(base, BW)
            below = pl.ds(base + BW, BW)
            u_col = kept[s, slot_of(jnp.where(following == k + 1, k, -1000))]
            b_before = beneath[s]
            u_row = rows[s, 0:1, :]
            u_before = rows[s, 1:2, :]
            u_head = rows[s, 2:3, :]
            corner = rows[s, 3:4, :]

            low = lefts[s][below, :]
            if s > 0:
                other = rows[s - 1, 3:4, :]
                patch = jnp.where(line == s - 1, other, left_over(s - 1, k == steps - 2))
                low = jnp.where(sub == BW - 1, patch, low)
            b = lane_sum(low * u_row)
            pick = jnp.where(following == 0, (s - 1) % BW, s)
            first = lane_sum(jnp.where(lane == pick, low, 0.0))
            b = spread(b)
            x_col = spread(first) - b * u_head
            x_row = row_sum(jnp.where(turn == s, x_col, 0.0))
            x_head = x_col[0:1, :]
            rest_row = jnp.where(line == s, 0.0, x_row)
            rest = spread(lane_sum(rest_row * rest_row))
            length = jnp.sqrt(rest + x_head * x_head)
            head = x_head + length
            size = rest + head * head
            valid = (following >= 0) & (following < steps)
            scale = jnp.where(valid, jnp.sqrt(2.0 / size), 0.0)
            next_head = jnp.where(valid, scale * head, 0.0)
            next_row = scale * rest_row + jnp.where(line == s, next_head, 0.0)
            next_col = jnp.where(sub == 0, next_head, scale * x_col)
            next_corner = jnp.where(valid, -length, x_head)

            left = lefts[s][here, :] - b_before * u_before
            a_row = row_sum(u_col * left)
            left = left - u_col * a_row
            mid = diags[s][here, :]
            if s > 0:
                edge = lane_sum(jnp.where(turn == s, mid[BW - 1 : BW, :], 0.0))
                mid = jnp.where((lane == s - 1) & (sub < BW - 1), edge, mid)
            y_row = row_sum(u_col * mid)
            y_col = lane_sum(mid * u_row)
            half = 0.5 * lane_sum(u_row * y_row)
            z_row = y_row - half * u_row
            z_col = y_col - half * u_col
            mid = mid - u_col * z_row - z_col * u_row
            new_left = jnp.where(lane == s, mid, left)
            new_left = jnp.where(
                sub == 0, jnp.where(line == s, corner, left_over(s, k == steps)), new_left
            )
            new_mid = jnp.where((sub == 0) & (lane != s), left, mid)
            lefts[s + 1][here, :] = new_left
            diags[s + 1][here, :] = new_mid
            beneath[s] = b
            rows[s, 0:1, :] = next_row
            rows[s, 1:2, :] = u_row
            rows[s, 2:3, :] = next_head
            rows[s, 3:4, :] = next_corner
            kept[s, slot_of(following)] = next_col

            @pl.when(following == steps)
            def _():
                work[s] = x_col

            @pl.when(following == 1)
            def _():
                column = line == (s - 1) % BW
                cleared = jnp.where(column | (sub == 0), 0.0, new_left)
                lefts[s + 1][here, :] = cleared
                top = pl.ds(base, 1)
                diags[s + 1][top, :] = jnp.where(column, corner, new_mid[0:1, :])

        return carry

    lax.fori_loop(-1, steps + 2 * SWEEPS, stage, 0)

    count = band_out.shape[1]
    for block in range(count // BW):
        begin = device * count + block * BW
        low = lefts[4][pl.ds(begin + OFF, BW), :]
        mid = diags[4][pl.ds(begin + OFF, BW), :]
        row = begin + sub
        place_i = (row - (SWEEPS + 1)) & (BW - 1)
        place_j = (lane - SWEEPS) & (BW - 1)
        inner = jnp.where(place_j <= place_i, mid, low)
        outer = jnp.where(place_j <= place_i, low, 0.0)
        for s in range(SWEEPS):
            top = steps * BW + s + 1
            gap = (begin - top) & (BW - 1)
            tail = pltpu.roll(work[s], BW - gap, 0)
            inside = (row > steps * BW + SWEEPS) & (row < top + BW) & (lane == s)
            outer = jnp.where(inside, tail, outer)
        chosen = jnp.where(slice_index < SWEEPS * 2, inner, outer)
        chosen = pltpu.roll(chosen, 1, 1)
        for bit in range(7):
            step = 1 << bit
            chosen = jnp.where((sub & step) != 0, pltpu.roll(chosen, BW - step, 1), chosen)
        work[SWEEPS] = chosen.T
        for index in range(band_out.shape[0]):
            source = (-(slice_index * band_out.shape[0] + index)) & (BW - 1)
            band_out[index : index + 1, pl.ds(block * BW, BW)] = work[SWEEPS, pl.ds(source, 1), :]

    held = scratch[14]
    held[...] = slab[...]
    for s in reversed(range(SWEEPS)):
        for window in range(SWEEPS - 1 - s, SLOTS - 1):
            at = pl.ds(window * BW + s + 1, BW)
            block = held[at, :]
            u_col = kept[s, window]
            held[at, :] = block - u_col * row_sum(u_col * block)
    slab_out[...] = held[pl.ds(HALO, slab_out.shape[0]), :]


def run_chase(place, reversed_diags, last_diag, slab, band_shape, slab_shape):
    order = reversed_diags.shape[1]
    rows = (OFF + (order // BW + 7) * BW + 2 * BW) // 8 * 8
    vmem = pl.BlockSpec(memory_space=pltpu.VMEM)
    return pl.pallas_call(
        chase_kernel,
        out_shape=(
            jax.ShapeDtypeStruct(band_shape, jnp.float32),
            jax.ShapeDtypeStruct(slab_shape, jnp.float32),
        ),
        in_specs=[pl.BlockSpec(memory_space=pltpu.SMEM), vmem, vmem, vmem],
        out_specs=(vmem, vmem),
        scratch_shapes=[pltpu.VMEM((rows, BW), jnp.float32)] * 10
        + [
            pltpu.VMEM((SWEEPS, SLOTS, BW, BW), jnp.float32),
            pltpu.VMEM((SWEEPS, BW, BW), jnp.float32),
            pltpu.VMEM((SWEEPS, 8, BW), jnp.float32),
            pltpu.VMEM((SWEEPS + 1, BW, BW), jnp.float32),
            pltpu.VMEM((HALO + slab_shape[0] + TAIL, slab_shape[1]), jnp.float32),
        ],
        compiler_params=pltpu.CompilerParams(vmem_limit_bytes=60 << 20),
    )(place, reversed_diags, last_diag, slab)


def body(band_diagonals, eigenvectors):
    device = lax.axis_index("band")
    column = lax.axis_index("cols")
    rows_dev, columns = eigenvectors.shape
    devices = lax.axis_size("band")
    order = rows_dev * devices
    up = lambda by: [(i, i + by) for i in range(devices) if 0 <= i + by < devices]
    above_1 = lax.ppermute(eigenvectors, "band", up(1))
    above_2 = lax.ppermute(eigenvectors[rows_dev - (HALO - rows_dev) :], "band", up(2))
    beyond = lax.ppermute(eigenvectors[:TAIL], "band", up(-1))
    slab = jnp.concatenate([above_2, above_1, eigenvectors, beyond], 0)

    pieces = lax.all_gather(band_diagonals, "cols", axis=0, tiled=True)[: BW + 8]
    pieces = lax.all_gather(pieces, "band", axis=1, tiled=True)
    reversed_diags = pieces[:BW][::-1]
    last_diag = pieces[BW : BW + 8]
    place = jnp.stack([device, column]).astype(jnp.int32)

    return run_chase(place, reversed_diags, last_diag, slab, band_diagonals.shape, eigenvectors.shape)


def solution(mesh):
    return jax.shard_map(
        body,
        mesh=mesh,
        in_specs=(P("cols", "band"), P("band", "cols")),
        out_specs=(P("cols", "band"), P("band", "cols")),
        check_vma=False,
    )
```

```python
import jax
import jax.numpy as jnp
from jax import lax
from jax.experimental import pallas as pl
from jax.experimental.pallas import tpu as pltpu
from jax.sharding import PartitionSpec as P

SWEEPS = 4
BW = 128
OFF = 255
HALO = 512
TAIL = 8
SLOTS = 8


def lane_sum(x):
    return jnp.sum(x, axis=1, keepdims=True)


def row_sum(x):
    return jnp.sum(x, axis=0, keepdims=True)


def spread(x):
    return jnp.broadcast_to(x, (x.shape[0], BW))


def chase_kernel(place, segments, slab, band_out, slab_out, *scratch):
    lefts = scratch[0:5]
    diags = scratch[5:10]
    beneath, rows, work, held = scratch[10:14]
    kept = scratch[14:18]
    segment = segments.shape[2] // BW
    order = segments.shape[0] * segments.shape[2]
    steps = order // BW - 2
    device, slice_index = place[0], place[1]
    first_window = (device * slab_out.shape[0]) // BW - HALO // BW

    lane = lax.broadcasted_iota(jnp.int32, (BW, BW), 1)
    sub = lax.broadcasted_iota(jnp.int32, (BW, BW), 0)
    line = lax.broadcasted_iota(jnp.int32, (1, BW), 1)
    turn = (lane - sub) & (BW - 1)

    zero_block = jnp.zeros((BW, BW), jnp.float32)
    for ref in lefts + diags:
        for block in range(4):
            ref[pl.ds(block * BW, BW), :] = zero_block
    for ref in (lefts[0], diags[0]):
        start = (order + OFF) // 8 * 8
        ref[pl.ds(start, ref.shape[0] - start), :] = jnp.zeros((ref.shape[0] - start, BW), jnp.float32)
    for s in range(SWEEPS):
        beneath[s] = zero_block
        rows[s] = jnp.zeros((8, BW), jnp.float32)
        for slot in range(SLOTS):
            kept[s][slot] = zero_block

    own = (sub - 1) & (BW - 1)

    def lay_out(block, carry):
        begin = pl.multiple_of(block * BW, BW)
        source = pl.ds(pl.multiple_of((block % segment) * BW, BW), BW)
        tile = segments[block // segment, 0:BW, source].T
        tile = pltpu.roll(tile, 0, 1, stride=1, stride_axis=0)
        far = pltpu.roll(segments[block // segment, BW : BW + 8, source], BW - 1, 1)
        far = jnp.broadcast_to(far[7:8, :], (BW, BW))
        left = jnp.where(lane > own, tile, jnp.where(lane == own, far, 0.0))
        lefts[0][pl.ds(begin + OFF, BW), :] = left
        diags[0][pl.ds(begin + OFF, BW), :] = jnp.where(lane <= own, tile, 0.0)
        return carry

    lax.fori_loop(0, order // BW, lay_out, 0)

    def mirror(block, carry):
        at = pl.ds(pl.multiple_of(block * BW, 8), BW)
        lower = diags[0][at, :]
        diags[0][at, :] = jnp.where(lane <= sub, lower, lower.T)
        return carry

    lax.fori_loop(1, order // BW + 2, mirror, 0)

    def slot_of(window):
        index = window - first_window
        return jnp.where((index >= 0) & (index < SLOTS - 1), index, SLOTS - 1)

    def left_over(s, last):
        entries = jnp.zeros((1, BW), jnp.float32)
        for back in range(1, s + 1):
            entry = work[s - back, back : back + 1, :]
            entries = jnp.where((line == s - back) & last, entry, entries)
        return entries

    def stage(t, carry):
        for s in reversed(range(SWEEPS)):
            k = jnp.maximum(t - 2 * s, -1)
            following = t - 2 * s + 1
            base = k * BW + (s + 1 + OFF)
            here = pl.ds(base, BW)
            below = pl.ds(base + BW, BW)
            u_col = kept[s][slot_of(jnp.where(following == k + 1, k, -1000))]
            b_before = beneath[s]
            u_row = rows[s, 0:1, :]
            u_before = rows[s, 1:2, :]
            u_head = rows[s, 2:3, :]
            corner = rows[s, 3:4, :]

            low = lefts[s][below, :]
            if s > 0:
                other = rows[s - 1, 3:4, :]
                patch = jnp.where(line == s - 1, other, left_over(s - 1, k == steps - 2))
                low = jnp.where(sub == BW - 1, patch, low)
            b = lane_sum(low * u_row)
            pick = jnp.where(following == 0, (s - 1) % BW, s)
            first = lane_sum(jnp.where(lane == pick, low, 0.0))
            b = spread(b)
            x_col = spread(first) - b * u_head
            x_row = row_sum(jnp.where(turn == s, x_col, 0.0))
            x_head = x_col[0:1, :]
            rest_row = jnp.where(line == s, 0.0, x_row)
            rest = spread(lane_sum(rest_row * rest_row))
            length = jnp.sqrt(rest + x_head * x_head)
            head = x_head + length
            size = rest + head * head
            valid = (following >= 0) & (following < steps)
            scale = jnp.where(valid, jnp.sqrt(2.0 / size), 0.0)
            next_head = jnp.where(valid, scale * head, 0.0)
            next_row = scale * rest_row + jnp.where(line == s, next_head, 0.0)
            next_col = jnp.where(sub == 0, next_head, scale * x_col)
            next_corner = jnp.where(valid, -length, x_head)

            left = lefts[s][here, :] - b_before * u_before
            a_row = row_sum(u_col * left)
            left = left - u_col * a_row
            mid = diags[s][here, :]
            if s > 0:
                edge = lane_sum(jnp.where(turn == s, mid[BW - 1 : BW, :], 0.0))
                mid = jnp.where((lane == s - 1) & (sub < BW - 1), edge, mid)
            y_row = row_sum(u_col * mid)
            y_col = lane_sum(mid * u_row)
            half = 0.5 * lane_sum(u_row * y_row)
            z_row = y_row - half * u_row
            z_col = y_col - half * u_col
            mid = mid - u_col * z_row - z_col * u_row
            new_left = jnp.where(lane == s, mid, left)
            new_left = jnp.where(
                sub == 0, jnp.where(line == s, corner, left_over(s, k == steps)), new_left
            )
            new_mid = jnp.where((sub == 0) & (lane != s), left, mid)
            lefts[s + 1][here, :] = new_left
            diags[s + 1][here, :] = new_mid
            beneath[s] = b
            rows[s, 0:1, :] = next_row
            rows[s, 1:2, :] = u_row
            rows[s, 2:3, :] = next_head
            rows[s, 3:4, :] = next_corner
            kept[s][slot_of(following)] = next_col
            rows[s, 4:5, :] = corner

        @pl.when((t < 2 * SWEEPS) | (t >= steps - 1))
        def _():
            for s in range(SWEEPS):
                base = jnp.maximum(t - 2 * s, -1) * BW + (s + 1 + OFF)

                @pl.when(t - 2 * s == steps - 1)
                def _():
                    low = lefts[s][pl.ds(base + BW, BW), :]
                    low = jnp.where((lane == s) & (sub < BW - 1 + (s == 0)), low, 0.0)
                    head = lane_sum(jnp.where(line == s, rows[s, 1:2, :], 0.0))
                    work[s] = spread(lane_sum(low)) - beneath[s] * head

                @pl.when(t == 2 * s)
                def _():
                    column = line == (s - 1) % BW
                    at = pl.ds(base, BW)
                    left = lefts[s + 1][at, :]
                    lefts[s + 1][at, :] = jnp.where(column | (sub == 0), 0.0, left)
                    top = pl.ds(base, 1)
                    diags[s + 1][top, :] = jnp.where(column, rows[s, 4:5, :], diags[s + 1][top, :])

        return carry

    lax.fori_loop(-1, steps + 2 * SWEEPS, stage, 0)

    count = band_out.shape[1]
    for block in range(count // BW):
        begin = device * count + block * BW
        low = lefts[4][pl.ds(begin + OFF, BW), :]
        mid = diags[4][pl.ds(begin + OFF, BW), :]
        row = begin + sub
        place_i = (row - (SWEEPS + 1)) & (BW - 1)
        place_j = (lane - SWEEPS) & (BW - 1)
        inner = jnp.where(place_j <= place_i, mid, low)
        outer = jnp.where(place_j <= place_i, low, 0.0)
        for s in range(SWEEPS):
            top = steps * BW + s + 1
            gap = (begin - top) & (BW - 1)
            tail = pltpu.roll(work[s], BW - gap, 0)
            inside = (row > steps * BW + SWEEPS) & (row < top + BW) & (lane == s)
            outer = jnp.where(inside, tail, outer)
        chosen = jnp.where(slice_index < SWEEPS * 2, inner, outer)
        chosen = pltpu.roll(chosen, 1, 1)
        for bit in range(7):
            step = 1 << bit
            chosen = jnp.where((sub & step) != 0, pltpu.roll(chosen, BW - step, 1), chosen)
        work[SWEEPS] = chosen.T
        for index in range(band_out.shape[0]):
            source = (-(slice_index * band_out.shape[0] + index)) & (BW - 1)
            band_out[index : index + 1, pl.ds(block * BW, BW)] = work[SWEEPS, pl.ds(source, 1), :]

    held[...] = slab[...]
    for s in reversed(range(SWEEPS)):
        for window in range(SWEEPS - 1 - s, SLOTS - 1):
            at = pl.ds(window * BW + s + 1, BW)
            block = held[at, :]
            u_col = kept[s][window]
            held[at, :] = block - u_col * row_sum(u_col * block)
    slab_out[...] = held[pl.ds(HALO, slab_out.shape[0]), :]


def run_chase(place, segments, slab, band_shape, slab_shape):
    order = segments.shape[0] * segments.shape[2]
    rows = (OFF + (order // BW + 7) * BW + 2 * BW) // 8 * 8
    vmem = pl.BlockSpec(memory_space=pltpu.VMEM)
    return pl.pallas_call(
        chase_kernel,
        out_shape=(
            jax.ShapeDtypeStruct(band_shape, jnp.float32),
            jax.ShapeDtypeStruct(slab_shape, jnp.float32),
        ),
        in_specs=[pl.BlockSpec(memory_space=pltpu.SMEM), vmem, vmem],
        out_specs=(vmem, vmem),
        scratch_shapes=[pltpu.VMEM((rows, BW), jnp.float32)] * 10
        + [
            pltpu.VMEM((SWEEPS, BW, BW), jnp.float32),
            pltpu.VMEM((SWEEPS, 8, BW), jnp.float32),
            pltpu.VMEM((SWEEPS + 1, BW, BW), jnp.float32),
            pltpu.VMEM((HALO + slab_shape[0] + TAIL, slab_shape[1]), jnp.float32),
        ]
        + [pltpu.VMEM((SLOTS, BW, BW), jnp.float32)] * SWEEPS,
        compiler_params=pltpu.CompilerParams(vmem_limit_bytes=60 << 20),
    )(place, segments, slab)


def body(band_diagonals, eigenvectors):
    device = lax.axis_index("band")
    column = lax.axis_index("cols")
    rows_dev, columns = eigenvectors.shape
    devices = lax.axis_size("band")
    order = rows_dev * devices
    up = lambda by: [(i, i + by) for i in range(devices) if 0 <= i + by < devices]
    above_1 = lax.ppermute(eigenvectors, "band", up(1))
    above_2 = lax.ppermute(eigenvectors[rows_dev - (HALO - rows_dev) :], "band", up(2))
    beyond = lax.ppermute(eigenvectors[:TAIL], "band", up(-1))
    slab = jnp.concatenate([above_2, above_1, eigenvectors, beyond], 0)

    peers = lax.axis_size("cols")
    turned = band_diagonals[::-1]
    pieces = lax.all_to_all(jnp.broadcast_to(turned[None], (peers, *turned.shape)), "cols", 0, 0, tiled=True)
    count = BW // turned.shape[0]
    parts = [pieces[i] for i in reversed(range(count))] + [pieces[count, -8:]]
    segments = lax.all_gather(jnp.concatenate(parts, 0), "band", axis=0)
    place = jnp.stack([device, column]).astype(jnp.int32)

    return run_chase(place, segments, slab, band_diagonals.shape, eigenvectors.shape)


def solution(mesh):
    return jax.shard_map(
        body,
        mesh=mesh,
        in_specs=(P("cols", "band"), P("band", "cols")),
        out_specs=(P("cols", "band"), P("band", "cols")),
        check_vma=False,
    )
```

```python
import functools

import jax
import jax.numpy as jnp
from jax import lax
from jax.experimental import pallas as pl
from jax.experimental.pallas import tpu as pltpu
from jax.sharding import PartitionSpec as P

SWEEPS = 4
BW = 128
OFF = 255
HALO = 512
TAIL = 8
SLOTS = 8


def lane_sum(x):
    return jnp.sum(x, axis=1, keepdims=True)


def row_sum(x):
    return jnp.sum(x, axis=0, keepdims=True)


def spread(x):
    return jnp.broadcast_to(x, (x.shape[0], BW))


def in_three(x):
    high = x.astype(jnp.bfloat16).astype(jnp.float32)
    rest = x - high
    middle = rest.astype(jnp.bfloat16).astype(jnp.float32)
    return high, middle, rest - middle


def fill(index, base, values):
    for places, value in values:
        mask = index == places[0]
        for place in places[1:]:
            mask = mask | (index == place)
        base = jnp.where(mask, value, base)
    return base


def outer_sum(u, y, entering, unit):
    index = lax.broadcasted_iota(jnp.int32, (16, BW), 0)
    u1, u2, u3 = in_three(u)
    left = fill(index, jnp.zeros((16, BW), jnp.float32), [((0, 1, 2), u1), ((3, 4), u2), ((5,), u3)])
    right = fill(index, jnp.zeros((16, BW), jnp.float32), [((6, 7, 8), u1), ((9, 10), u2), ((11,), u3)])
    if entering is not None:
        e1, e2, e3 = in_three(entering)
        left = fill(index, left, [((12,), e1), ((13,), e2), ((14,), e3)])
        right = fill(index, right, [((12, 13, 14), unit)])
    y1, y2, y3 = in_three(y)
    left = fill(index, left, [((6, 9, 11), y1), ((7, 10), y2), ((8,), y3)])
    right = fill(index, right, [((0, 3, 5), y1), ((1, 4), y2), ((2,), y3)])
    return lax.dot_general(
        left.astype(jnp.bfloat16),
        right.astype(jnp.bfloat16),
        (((0,), (0,)), ((), ())),
        preferred_element_type=jnp.float32,
    )


def chase_kernel(kinds, *refs):
    place, slab = refs[0:2]
    parts = refs[2 : 2 + len(kinds)]
    band_out, slab_out = refs[2 + len(kinds) : 4 + len(kinds)]
    scratch = refs[4 + len(kinds) :]
    lefts = scratch[0:5]
    diags = scratch[5:10]
    beneath, rows, work, held, turned = scratch[10:15]
    kept = scratch[15:19]
    order = kinds[0][3]
    steps = order // BW - 2
    device, slice_index = place[0], place[1]
    first_window = (device * slab_out.shape[0]) // BW - HALO // BW

    lane = lax.broadcasted_iota(jnp.int32, (BW, BW), 1)
    sub = lax.broadcasted_iota(jnp.int32, (BW, BW), 0)
    line = lax.broadcasted_iota(jnp.int32, (1, BW), 1)
    turn = (lane - sub) & (BW - 1)

    zero_block = jnp.zeros((BW, BW), jnp.float32)
    for ref in lefts + diags:
        for block in range(4):
            ref[pl.ds(block * BW, BW), :] = zero_block
    for ref in (lefts[0], diags[0]):
        start = (order + OFF) // 8 * 8
        ref[pl.ds(start, ref.shape[0] - start), :] = jnp.zeros((ref.shape[0] - start, BW), jnp.float32)
    for s in range(SWEEPS):
        beneath[s] = zero_block
        rows[s] = jnp.zeros((8, BW), jnp.float32)
        for slot in range(SLOTS):
            kept[s][slot] = zero_block

    own = (sub - 1) & (BW - 1)

    for part, (core, side, first, _) in zip(parts, kinds):
        length = part.shape[2]

        def lay_out(index, carry):
            owner = (index + first) * 4 + ((device & 3) ^ (2 * side + core))
            for block in range(length // BW):
                source = pl.ds(block * BW, BW)
                begin = pl.multiple_of(owner * length + block * BW, BW) + OFF
                tile = part[index, 0:BW, source].T
                tile = pltpu.roll(tile, 0, 1, stride=1, stride_axis=0)
                far = pltpu.roll(part[index, BW : BW + 8, source], BW - 1, 1)
                far = jnp.broadcast_to(far[7:8, :], (BW, BW))
                left = jnp.where(lane > own, tile, jnp.where(lane == own, far, 0.0))
                lefts[0][pl.ds(begin, BW), :] = left
                diags[0][pl.ds(begin, BW), :] = jnp.where(lane <= own, tile, 0.0)
            return carry

        lax.fori_loop(0, part.shape[0], lay_out, 0)

    def mirror(index, carry):
        places = [pl.ds(pl.multiple_of((index * 7 + i) * BW + BW, 8), BW) for i in range(7)]
        lowers = [diags[0][at, :] for at in places]
        for at, lower in zip(places, lowers):
            diags[0][at, :] = jnp.where(lane <= sub, lower, lower.T)
        return carry

    lax.fori_loop(0, (order // BW + 1) // 7, mirror, 0)

    def slot_of(window):
        index = window - first_window
        return jnp.where((index >= 0) & (index < SLOTS - 1), index, SLOTS - 1)

    def left_over(s, last):
        entries = jnp.zeros((1, BW), jnp.float32)
        for back in range(1, s + 1):
            entry = work[s - back, back : back + 1, :]
            entries = jnp.where((line == s - back) & last, entry, entries)
        return entries

    def stage(t, carry):
        for s in reversed(range(SWEEPS)):
            k = jnp.maximum(t - 2 * s, -1)
            following = t - 2 * s + 1
            base = k * BW + (s + 1 + OFF)
            here = pl.ds(base, BW)
            below = pl.ds(base + BW, BW)
            u_col = kept[s][slot_of(jnp.where(following == k + 1, k, -1000))]
            b_before = beneath[s]
            u_row = rows[s, 0:1, :]
            u_before = rows[s, 1:2, :]
            u_head = rows[s, 2:3, :]
            corner = rows[s, 3:4, :]

            low = lefts[s][below, :]
            if s > 0:
                other = rows[s - 1, 3:4, :]
                patch = jnp.where(line == s - 1, other, left_over(s - 1, k == steps - 2))
                low = jnp.where(sub == BW - 1, patch, low)
            b = lane_sum(low * u_row)
            pick = jnp.where(following == 0, (s - 1) % BW, s)
            first = lane_sum(jnp.where(lane == pick, low, 0.0))
            b = spread(b)
            x_col = spread(first) - b * u_head
            x_row = row_sum(jnp.where(turn == s, x_col, 0.0))
            x_head = x_col[0:1, :]
            rest_row = jnp.where(line == s, 0.0, x_row)
            rest_col = jnp.where(sub == 0, 0.0, x_col)
            rest = row_sum(rest_col * rest_col)
            length = jnp.sqrt(rest + x_head * x_head)
            head = x_head + length
            size = rest + head * head
            valid = (following >= 0) & (following < steps)
            scale = jnp.where(valid, lax.rsqrt(0.5 * size), 0.0)
            next_head = jnp.where(valid, scale * head, 0.0)
            next_row = scale * rest_row + jnp.where(line == s, next_head, 0.0)
            next_col = jnp.where(sub == 0, next_head, scale * x_col)
            next_corner = jnp.where(valid, -length, x_head)

            left = lefts[s][here, :] - b_before * u_before
            a_row = row_sum(u_col * left)
            left = left - u_col * a_row
            mid = diags[s][here, :]
            y_row = row_sum(u_col * mid)
            entering, unit = None, None
            if s > 0:
                last_row = mid[BW - 1 : BW, :]
                column = line == s - 1
                y_row = jnp.where(column, lane_sum(u_row * last_row), y_row)
                mid = jnp.where((lane == s - 1) & (sub < BW - 1), 0.0, mid)
                entering = jnp.where(column, 0.0, last_row)
                unit = jnp.where(column, -1.0, 0.0)
            product = lane_sum(u_row * y_row)
            change = outer_sum(u_row, y_row, entering, unit)
            if s > 0:
                turned[s, 0:BW, :] = change
                turned[s, BW : BW + 8, :] = change[0:8, :]
                change = turned[s, s : s + BW, :]
            mid = mid + u_col * (product * u_row) - change
            new_left = jnp.where(lane == s, mid, left)
            new_left = jnp.where(
                sub == 0, jnp.where(line == s, corner, left_over(s, k == steps)), new_left
            )
            new_mid = jnp.where((sub == 0) & (lane != s), left, mid)
            lefts[s + 1][here, :] = new_left
            diags[s + 1][here, :] = new_mid
            beneath[s] = b
            rows[s, 0:1, :] = next_row
            rows[s, 1:2, :] = u_row
            rows[s, 2:3, :] = next_head
            rows[s, 3:4, :] = next_corner
            kept[s][slot_of(following)] = next_col
            rows[s, 4:5, :] = corner

        @pl.when((t < 2 * SWEEPS) | (t >= steps - 1))
        def _():
            for s in range(SWEEPS):
                base = jnp.maximum(t - 2 * s, -1) * BW + (s + 1 + OFF)

                @pl.when(t - 2 * s == steps - 1)
                def _():
                    low = lefts[s][pl.ds(base + BW, BW), :]
                    low = jnp.where((lane == s) & (sub < BW - 1 + (s == 0)), low, 0.0)
                    head = lane_sum(jnp.where(line == s, rows[s, 1:2, :], 0.0))
                    work[s] = spread(lane_sum(low)) - beneath[s] * head

                @pl.when(t == 2 * s)
                def _():
                    column = line == (s - 1) % BW
                    at = pl.ds(base, BW)
                    left = lefts[s + 1][at, :]
                    lefts[s + 1][at, :] = jnp.where(column | (sub == 0), 0.0, left)
                    top = pl.ds(base, 1)
                    diags[s + 1][top, :] = jnp.where(column, rows[s, 4:5, :], diags[s + 1][top, :])

        return carry

    lax.fori_loop(-1, steps + 2 * SWEEPS, stage, 0)

    count = band_out.shape[1]
    for block in range(count // BW):
        begin = device * count + block * BW
        low = lefts[4][pl.ds(begin + OFF, BW), :]
        mid = diags[4][pl.ds(begin + OFF, BW), :]
        row = begin + sub
        place_i = (row - (SWEEPS + 1)) & (BW - 1)
        place_j = (lane - SWEEPS) & (BW - 1)
        inner = jnp.where(place_j <= place_i, mid, low)
        outer = jnp.where(place_j <= place_i, low, 0.0)
        for s in range(SWEEPS):
            top = steps * BW + s + 1
            gap = (begin - top) & (BW - 1)
            tail = pltpu.roll(work[s], BW - gap, 0)
            inside = (row > steps * BW + SWEEPS) & (row < top + BW) & (lane == s)
            outer = jnp.where(inside, tail, outer)
        chosen = jnp.where(slice_index < SWEEPS * 2, inner, outer)
        chosen = pltpu.roll(chosen, 1, 1)
        for bit in range(7):
            step = 1 << bit
            chosen = jnp.where((sub & step) != 0, pltpu.roll(chosen, BW - step, 1), chosen)
        work[SWEEPS] = chosen.T
        for index in range(band_out.shape[0]):
            source = (-(slice_index * band_out.shape[0] + index)) & (BW - 1)
            band_out[index : index + 1, pl.ds(block * BW, BW)] = work[SWEEPS, pl.ds(source, 1), :]

    held[...] = slab[...]
    for s in reversed(range(SWEEPS)):
        for window in range(SWEEPS - 1 - s, SLOTS - 1):
            at = pl.ds(window * BW + s + 1, BW)
            block = held[at, :]
            u_col = kept[s][window]
            held[at, :] = block - u_col * row_sum(u_col * block)
    slab_out[...] = held[pl.ds(HALO, slab_out.shape[0]), :]


def run_chase(place, slab, parts, kinds, band_shape, slab_shape):
    order = kinds[0][3]
    rows = (OFF + (order // BW + 7) * BW + 2 * BW) // 8 * 8
    vmem = pl.BlockSpec(memory_space=pltpu.VMEM)
    return pl.pallas_call(
        functools.partial(chase_kernel, kinds),
        out_shape=(
            jax.ShapeDtypeStruct(band_shape, jnp.float32),
            jax.ShapeDtypeStruct(slab_shape, jnp.float32),
        ),
        in_specs=[pl.BlockSpec(memory_space=pltpu.SMEM)] + [vmem] * (1 + len(parts)),
        out_specs=(vmem, vmem),
        scratch_shapes=[pltpu.VMEM((rows, BW), jnp.float32)] * 10
        + [
            pltpu.VMEM((SWEEPS, BW, BW), jnp.float32),
            pltpu.VMEM((SWEEPS, 8, BW), jnp.float32),
            pltpu.VMEM((SWEEPS + 1, BW, BW), jnp.float32),
            pltpu.VMEM((HALO + slab_shape[0] + TAIL, slab_shape[1]), jnp.float32),
            pltpu.VMEM((SWEEPS, BW + 8, BW), jnp.float32),
        ]
        + [pltpu.VMEM((SLOTS, BW, BW), jnp.float32)] * SWEEPS,
        compiler_params=pltpu.CompilerParams(vmem_limit_bytes=60 << 20),
    )(place, slab, *parts)


def body(band_diagonals, eigenvectors):
    device = lax.axis_index("band")
    column = lax.axis_index("cols")
    rows_dev, columns = eigenvectors.shape
    devices = lax.axis_size("band")
    order = rows_dev * devices
    up = lambda by: [(i, i + by) for i in range(devices) if 0 <= i + by < devices]
    above_1 = lax.ppermute(eigenvectors, "band", up(1))
    above_2 = lax.ppermute(eigenvectors[rows_dev - (HALO - rows_dev) :], "band", up(2))
    beyond = lax.ppermute(eigenvectors[:TAIL], "band", up(-1))
    slab = jnp.concatenate([above_2, above_1, eigenvectors, beyond], 0)

    peers = lax.axis_size("cols")
    turned = band_diagonals[::-1]
    pieces = lax.all_to_all(jnp.broadcast_to(turned[None], (peers, *turned.shape)), "cols", 0, 0, tiled=True)
    count = BW // turned.shape[0]
    parts = [pieces[i] for i in reversed(range(count))] + [pieces[count, -8:]]
    own_part = jnp.concatenate(parts, 0)
    quarter = devices // 4
    groups = [[y * 4 + i for y in range(quarter)] for i in range(4)]
    part_y = lax.all_gather(own_part, "band", axis=0, axis_index_groups=groups)

    def swap(x, band_bits, cols_bits):
        pairs = [
            (i * peers + j, (i ^ band_bits) * peers + (j ^ cols_bits))
            for i in range(devices)
            for j in range(peers)
        ]
        return lax.ppermute(x, ("band", "cols"), pairs)

    half = quarter // 2
    part_a = swap(part_y[:half], 2, 0)
    part_b = swap(part_y[half:], 2, peers // 2)
    parts = [part_y, part_a, part_b]
    parts += [swap(part, 1, 0) for part in parts]
    kinds = [(core, side, first, order) for core in (0, 1) for side, first in ((0, 0), (1, 0), (1, half))]
    place = jnp.stack([device, column]).astype(jnp.int32)

    return run_chase(place, slab, parts, kinds, band_diagonals.shape, eigenvectors.shape)


def solution(mesh):
    return jax.shard_map(
        body,
        mesh=mesh,
        in_specs=(P("cols", "band"), P("band", "cols")),
        out_specs=(P("cols", "band"), P("band", "cols")),
        check_vma=False,
    )
```

```python
import functools

import jax
import jax.numpy as jnp
from jax import lax
from jax.experimental import pallas as pl
from jax.experimental.pallas import tpu as pltpu
from jax.sharding import PartitionSpec as P

SWEEPS = 4
BW = 128
OFF = 255
HALO = 512
TAIL = 8
SLOTS = 8


def lane_sum(x):
    return jnp.sum(x, axis=1, keepdims=True)


def row_sum(x):
    return jnp.sum(x, axis=0, keepdims=True)


def spread(x):
    return jnp.broadcast_to(x, (x.shape[0], BW))


def in_three(x):
    high = x.astype(jnp.bfloat16).astype(jnp.float32)
    rest = x - high
    middle = rest.astype(jnp.bfloat16).astype(jnp.float32)
    return high, middle, rest - middle


def fill(index, base, values):
    for places, value in values:
        mask = index == places[0]
        for place in places[1:]:
            mask = mask | (index == place)
        base = jnp.where(mask, value, base)
    return base


def outer_sum(u, y, entering, unit):
    index = lax.broadcasted_iota(jnp.int32, (16, BW), 0)
    u1, u2, u3 = in_three(u)
    left = fill(index, jnp.zeros((16, BW), jnp.float32), [((0, 1, 2), u1), ((3, 4), u2), ((5,), u3)])
    right = fill(index, jnp.zeros((16, BW), jnp.float32), [((6, 7, 8), u1), ((9, 10), u2), ((11,), u3)])
    if entering is not None:
        e1, e2, e3 = in_three(entering)
        left = fill(index, left, [((12,), e1), ((13,), e2), ((14,), e3)])
        right = fill(index, right, [((12, 13, 14), unit)])
    y1, y2, y3 = in_three(y)
    left = fill(index, left, [((6, 9, 11), y1), ((7, 10), y2), ((8,), y3)])
    right = fill(index, right, [((0, 3, 5), y1), ((1, 4), y2), ((2,), y3)])
    return lax.dot_general(
        left.astype(jnp.bfloat16),
        right.astype(jnp.bfloat16),
        (((0,), (0,)), ((), ())),
        preferred_element_type=jnp.float32,
    )


def chase_kernel(kinds, *refs):
    place, slabs = refs[0], refs[1:5]
    parts = refs[5 : 5 + len(kinds)]
    band_out, slab_out = refs[5 + len(kinds) : 7 + len(kinds)]
    scratch = refs[7 + len(kinds) :]
    lefts = scratch[0:5]
    diags = scratch[5:10]
    beneath, rows, work, held, turned = scratch[10:15]
    kept = scratch[15:19]
    order = kinds[0][3]
    steps = order // BW - 2
    device, slice_index = place[0], place[1]
    first_window = (device * slab_out.shape[0]) // BW - HALO // BW

    lane = lax.broadcasted_iota(jnp.int32, (BW, BW), 1)
    sub = lax.broadcasted_iota(jnp.int32, (BW, BW), 0)
    line = lax.broadcasted_iota(jnp.int32, (1, BW), 1)
    turn = (lane - sub) & (BW - 1)

    zero_block = jnp.zeros((BW, BW), jnp.float32)
    for ref in lefts + diags:
        for block in range(4):
            ref[pl.ds(block * BW, BW), :] = zero_block
    for ref in (lefts[0], diags[0]):
        start = (order + OFF) // 8 * 8
        ref[pl.ds(start, ref.shape[0] - start), :] = jnp.zeros((ref.shape[0] - start, BW), jnp.float32)
    for s in range(SWEEPS):
        beneath[s] = zero_block
        rows[s] = jnp.zeros((8, BW), jnp.float32)
        for slot in range(SLOTS):
            kept[s][slot] = zero_block

    own = (sub - 1) & (BW - 1)

    for part, (core, side, first, _) in zip(parts, kinds):
        length = part.shape[2]

        def lay_out(index, carry):
            owner = (index + first) * 4 + ((device & 3) ^ (2 * side + core))
            for block in range(length // BW):
                source = pl.ds(block * BW, BW)
                begin = pl.multiple_of(owner * length + block * BW, BW) + OFF
                tile = part[index, 0:BW, source].T
                tile = pltpu.roll(tile, 0, 1, stride=1, stride_axis=0)
                far = pltpu.roll(part[index, BW : BW + 8, source], BW - 1, 1)
                far = jnp.broadcast_to(far[7:8, :], (BW, BW))
                left = jnp.where(lane > own, tile, jnp.where(lane == own, far, 0.0))
                lefts[0][pl.ds(begin, BW), :] = left
                diags[0][pl.ds(begin, BW), :] = jnp.where(lane <= own, tile, 0.0)
            return carry

        lax.fori_loop(0, part.shape[0], lay_out, 0)

    def mirror(index, carry):
        places = [pl.ds(pl.multiple_of((index * 7 + i) * BW + BW, 8), BW) for i in range(7)]
        lowers = [diags[0][at, :] for at in places]
        for at, lower in zip(places, lowers):
            diags[0][at, :] = jnp.where(lane <= sub, lower, lower.T)
        return carry

    lax.fori_loop(0, (order // BW + 1) // 7, mirror, 0)

    def slot_of(window):
        index = window - first_window
        return jnp.where((index >= 0) & (index < SLOTS - 1), index, SLOTS - 1)

    def left_over(s, last):
        entries = jnp.zeros((1, BW), jnp.float32)
        for back in range(1, s + 1):
            entry = work[s - back, back : back + 1, :]
            entries = jnp.where((line == s - back) & last, entry, entries)
        return entries

    def stage(t, carry):
        for s in reversed(range(SWEEPS)):
            k = jnp.maximum(t - 2 * s, -1)
            following = t - 2 * s + 1
            base = k * BW + (s + 1 + OFF)
            here = pl.ds(base, BW)
            below = pl.ds(base + BW, BW)
            u_col = kept[s][slot_of(jnp.where(following == k + 1, k, -1000))]
            b_before = beneath[s]
            u_row = rows[s, 0:1, :]
            u_before = rows[s, 1:2, :]
            u_head = rows[s, 2:3, :]
            corner = rows[s, 3:4, :]

            low = lefts[s][below, :]
            if s > 0:
                other = rows[s - 1, 3:4, :]
                patch = jnp.where(line == s - 1, other, left_over(s - 1, k == steps - 2))
                low = jnp.where(sub == BW - 1, patch, low)
            b = lane_sum(low * u_row)
            pick = jnp.where(following == 0, (s - 1) % BW, s)
            first = lane_sum(jnp.where(lane == pick, low, 0.0))
            b = spread(b)
            x_col = spread(first) - b * u_head
            x_row = row_sum(jnp.where(turn == s, x_col, 0.0))
            x_head = x_col[0:1, :]
            rest_row = jnp.where(line == s, 0.0, x_row)
            rest_col = jnp.where(sub == 0, 0.0, x_col)
            rest = row_sum(rest_col * rest_col)
            length = jnp.sqrt(rest + x_head * x_head)
            head = x_head + length
            size = rest + head * head
            valid = (following >= 0) & (following < steps)
            scale = jnp.where(valid, lax.rsqrt(0.5 * size), 0.0)
            next_head = jnp.where(valid, scale * head, 0.0)
            next_row = scale * rest_row + jnp.where(line == s, next_head, 0.0)
            next_col = jnp.where(sub == 0, next_head, scale * x_col)
            next_corner = jnp.where(valid, -length, x_head)

            left = lefts[s][here, :] - b_before * u_before
            a_row = row_sum(u_col * left)
            left = left - u_col * a_row
            mid = diags[s][here, :]
            y_row = row_sum(u_col * mid)
            entering, unit = None, None
            if s > 0:
                last_row = mid[BW - 1 : BW, :]
                column = line == s - 1
                y_row = jnp.where(column, lane_sum(u_row * last_row), y_row)
                mid = jnp.where((lane == s - 1) & (sub < BW - 1), 0.0, mid)
                entering = jnp.where(column, 0.0, last_row)
                unit = jnp.where(column, -1.0, 0.0)
            product = lane_sum(u_row * y_row)
            change = outer_sum(u_row, y_row, entering, unit)
            if s > 0:
                turned[s, 0:BW, :] = change
                turned[s, BW : BW + 8, :] = change[0:8, :]
                change = turned[s, s : s + BW, :]
            mid = mid + u_col * (product * u_row) - change
            new_left = jnp.where(lane == s, mid, left)
            new_left = jnp.where(
                sub == 0, jnp.where(line == s, corner, left_over(s, k == steps)), new_left
            )
            new_mid = jnp.where((sub == 0) & (lane != s), left, mid)
            lefts[s + 1][here, :] = new_left
            diags[s + 1][here, :] = new_mid
            beneath[s] = b
            rows[s, 0:1, :] = next_row
            rows[s, 1:2, :] = u_row
            rows[s, 2:3, :] = next_head
            rows[s, 3:4, :] = next_corner
            kept[s][slot_of(following)] = next_col
            rows[s, 4:5, :] = corner

        @pl.when((t < 2 * SWEEPS) | (t >= steps - 1))
        def _():
            for s in range(SWEEPS):
                base = jnp.maximum(t - 2 * s, -1) * BW + (s + 1 + OFF)

                @pl.when(t - 2 * s == steps - 1)
                def _():
                    low = lefts[s][pl.ds(base + BW, BW), :]
                    low = jnp.where((lane == s) & (sub < BW - 1 + (s == 0)), low, 0.0)
                    head = lane_sum(jnp.where(line == s, rows[s, 1:2, :], 0.0))
                    work[s] = spread(lane_sum(low)) - beneath[s] * head

                @pl.when(t == 2 * s)
                def _():
                    column = line == (s - 1) % BW
                    at = pl.ds(base, BW)
                    left = lefts[s + 1][at, :]
                    lefts[s + 1][at, :] = jnp.where(column | (sub == 0), 0.0, left)
                    top = pl.ds(base, 1)
                    diags[s + 1][top, :] = jnp.where(column, rows[s, 4:5, :], diags[s + 1][top, :])

        return carry

    lax.fori_loop(-1, steps + 2 * SWEEPS, stage, 0)

    count = band_out.shape[1]
    for block in range(count // BW):
        begin = device * count + block * BW
        low = lefts[4][pl.ds(begin + OFF, BW), :]
        mid = diags[4][pl.ds(begin + OFF, BW), :]
        row = begin + sub
        place_i = (row - (SWEEPS + 1)) & (BW - 1)
        place_j = (lane - SWEEPS) & (BW - 1)
        inner = jnp.where(place_j <= place_i, mid, low)
        outer = jnp.where(place_j <= place_i, low, 0.0)
        for s in range(SWEEPS):
            top = steps * BW + s + 1
            gap = (begin - top) & (BW - 1)
            tail = pltpu.roll(work[s], BW - gap, 0)
            inside = (row > steps * BW + SWEEPS) & (row < top + BW) & (lane == s)
            outer = jnp.where(inside, tail, outer)
        chosen = jnp.where(slice_index < SWEEPS * 2, inner, outer)
        chosen = pltpu.roll(chosen, 1, 1)
        for bit in range(7):
            step = 1 << bit
            chosen = jnp.where((sub & step) != 0, pltpu.roll(chosen, BW - step, 1), chosen)
        work[SWEEPS] = chosen.T
        for index in range(band_out.shape[0]):
            source = (-(slice_index * band_out.shape[0] + index)) & (BW - 1)
            band_out[index : index + 1, pl.ds(block * BW, BW)] = work[SWEEPS, pl.ds(source, 1), :]

    begin = 0
    for slab in slabs:
        held[begin : begin + slab.shape[0], :] = slab[...]
        begin += slab.shape[0]
    for s in reversed(range(SWEEPS)):
        for window in range(SWEEPS - 1 - s, SLOTS - 1):
            at = pl.ds(window * BW + s + 1, BW)
            block = held[at, :]
            u_col = kept[s][window]
            held[at, :] = block - u_col * row_sum(u_col * block)
    slab_out[...] = held[pl.ds(HALO, slab_out.shape[0]), :]


def run_chase(place, slabs, parts, kinds, band_shape, slab_shape):
    order = kinds[0][3]
    rows = (OFF + (order // BW + 7) * BW + 2 * BW) // 8 * 8
    vmem = pl.BlockSpec(memory_space=pltpu.VMEM)
    return pl.pallas_call(
        functools.partial(chase_kernel, kinds),
        out_shape=(
            jax.ShapeDtypeStruct(band_shape, jnp.float32),
            jax.ShapeDtypeStruct(slab_shape, jnp.float32),
        ),
        in_specs=[pl.BlockSpec(memory_space=pltpu.SMEM)] + [vmem] * (len(slabs) + len(parts)),
        out_specs=(vmem, vmem),
        scratch_shapes=[pltpu.VMEM((rows, BW), jnp.float32)] * 10
        + [
            pltpu.VMEM((SWEEPS, BW, BW), jnp.float32),
            pltpu.VMEM((SWEEPS, 8, BW), jnp.float32),
            pltpu.VMEM((SWEEPS + 1, BW, BW), jnp.float32),
            pltpu.VMEM((HALO + slab_shape[0] + TAIL, slab_shape[1]), jnp.float32),
            pltpu.VMEM((SWEEPS, BW + 8, BW), jnp.float32),
        ]
        + [pltpu.VMEM((SLOTS, BW, BW), jnp.float32)] * SWEEPS,
        compiler_params=pltpu.CompilerParams(vmem_limit_bytes=60 << 20),
    )(place, *slabs, *parts)


def body(band_diagonals, eigenvectors):
    device = lax.axis_index("band")
    column = lax.axis_index("cols")
    rows_dev, columns = eigenvectors.shape
    devices = lax.axis_size("band")
    order = rows_dev * devices
    up = lambda by: [(i, i + by) for i in range(devices) if 0 <= i + by < devices]
    above_1 = lax.ppermute(eigenvectors, "band", up(1))
    above_2 = lax.ppermute(eigenvectors[rows_dev - (HALO - rows_dev) :], "band", up(2))
    beyond = lax.ppermute(eigenvectors[:TAIL], "band", up(-1))

    peers = lax.axis_size("cols")
    turned = band_diagonals[::-1]
    pieces = lax.all_to_all(jnp.broadcast_to(turned[None], (peers, *turned.shape)), "cols", 0, 0, tiled=True)
    pieces, above_1, above_2, beyond = lax.optimization_barrier((pieces, above_1, above_2, beyond))
    slabs = (above_2, above_1, eigenvectors, beyond)
    count = BW // turned.shape[0]
    parts = [pieces[i] for i in reversed(range(count))] + [pieces[count, -8:]]
    own_part = jnp.concatenate(parts, 0)
    quarter = devices // 4
    groups = [[y * 4 + i for y in range(quarter)] for i in range(4)]
    part_y = lax.all_gather(own_part, "band", axis=0, axis_index_groups=groups)

    def swap(x, band_bits, cols_bits):
        pairs = [
            (i * peers + j, (i ^ band_bits) * peers + (j ^ cols_bits))
            for i in range(devices)
            for j in range(peers)
        ]
        return lax.ppermute(x, ("band", "cols"), pairs)

    half = quarter // 2
    part_a = swap(part_y[:half], 2, 0)
    part_b = swap(part_y[half:], 2, peers // 2)
    parts = [part_y, part_a, part_b]
    parts += [swap(part, 1, 0) for part in parts]
    kinds = [(core, side, first, order) for core in (0, 1) for side, first in ((0, 0), (1, 0), (1, half))]
    place = jnp.stack([device, column]).astype(jnp.int32)

    return run_chase(place, slabs, parts, kinds, band_diagonals.shape, eigenvectors.shape)


def solution(mesh):
    return jax.shard_map(
        body,
        mesh=mesh,
        in_specs=(P("cols", "band"), P("band", "cols")),
        out_specs=(P("cols", "band"), P("band", "cols")),
        check_vma=False,
    )
```

```python
import functools

import jax
import jax.numpy as jnp
from jax import lax
from jax.experimental import pallas as pl
from jax.experimental.pallas import tpu as pltpu
from jax.sharding import PartitionSpec as P

SWEEPS = 4
BW = 128
OFF = 255
HALO = 512
TAIL = 8
SLOTS = 8


def lane_sum(x):
    return jnp.sum(x, axis=1, keepdims=True)


def row_sum(x):
    return jnp.sum(x, axis=0, keepdims=True)


def spread(x):
    return jnp.broadcast_to(x, (x.shape[0], BW))


def with_first(x, row):
    index = lax.broadcasted_iota(jnp.int32, (8, BW), 0)
    return jnp.concatenate([jnp.where(index == 0, row, x[:8]), x[8:]], 0)


def with_last(x, row):
    index = lax.broadcasted_iota(jnp.int32, (8, BW), 0)
    return jnp.concatenate([x[:-8], jnp.where(index == 7, row, x[-8:])], 0)


def tree_sum(terms):
    while len(terms) > 1:
        terms = [sum(terms[i : i + 2][1:], terms[i]) for i in range(0, len(terms), 2)]
    return terms[0]


def in_three(x):
    high = x.astype(jnp.bfloat16).astype(jnp.float32)
    rest = x - high
    middle = rest.astype(jnp.bfloat16).astype(jnp.float32)
    return high, middle, rest - middle


def fill(index, base, values):
    for places, value in values:
        mask = index == places[0]
        for place in places[1:]:
            mask = mask | (index == place)
        base = jnp.where(mask, value, base)
    return base


def outer_sum(u, y, entering, unit):
    index = lax.broadcasted_iota(jnp.int32, (16, BW), 0)
    zero = jnp.zeros((16, BW), jnp.float32)
    u1, u2, u3 = in_three(u)
    left, right = zero, fill(index, zero, [((0, 2, 5), u1), ((1, 3), u2), ((4,), u3)])
    if entering is not None:
        e1, e2, e3 = in_three(entering)
        left = fill(index, left, [((6,), e1), ((7,), e2), ((8,), e3)])
        right = fill(index, right, [((6, 7, 8), unit)])
    y1, y2, y3 = in_three(y)
    left = fill(index, left, [((0, 1, 4), y1), ((2, 3), y2), ((5,), y3)])
    return lax.dot_general(
        left.astype(jnp.bfloat16),
        right.astype(jnp.bfloat16),
        (((0,), (0,)), ((), ())),
        preferred_element_type=jnp.float32,
    )


def chase_kernel(kinds, *refs):
    place, slabs = refs[0], refs[1:5]
    parts = refs[5 : 5 + len(kinds)]
    band_out, slab_out = refs[5 + len(kinds) : 7 + len(kinds)]
    scratch = refs[7 + len(kinds) :]
    lefts = scratch[0:5]
    diags = scratch[5:10]
    rows, work, held, turned = scratch[10:14]
    kept = scratch[14:18]
    order = kinds[0][3]
    steps = order // BW - 2
    device, slice_index = place[0], place[1]
    first_window = (device * slab_out.shape[0]) // BW - HALO // BW

    lane = lax.broadcasted_iota(jnp.int32, (BW, BW), 1)
    sub = lax.broadcasted_iota(jnp.int32, (BW, BW), 0)
    line = lax.broadcasted_iota(jnp.int32, (1, BW), 1)
    turn8 = (lane[:8] - sub[:8]) & (BW - 1)

    zero_block = jnp.zeros((BW, BW), jnp.float32)
    for ref in lefts + diags:
        for block in range(4):
            ref[pl.ds(block * BW, BW), :] = zero_block
    for ref in (lefts[0], diags[0]):
        start = (order + OFF) // 8 * 8
        ref[pl.ds(start, ref.shape[0] - start), :] = jnp.zeros((ref.shape[0] - start, BW), jnp.float32)
    for s in range(SWEEPS):
        rows[s] = jnp.zeros((8, BW), jnp.float32)
        for slot in range(SLOTS):
            kept[s][slot] = zero_block

    own = (sub - 1) & (BW - 1)

    for part, (core, side, first, _) in zip(parts, kinds):
        length = part.shape[2]

        def lay_out(index, carry):
            owner = (index + first) * 4 + ((device & 3) ^ (2 * side + core))
            for block in range(length // BW):
                source = pl.ds(block * BW, BW)
                begin = pl.multiple_of(owner * length + block * BW, BW) + OFF
                tile = part[index, 0:BW, source].T
                tile = pltpu.roll(tile, 0, 1, stride=1, stride_axis=0)
                far = pltpu.roll(part[index, BW : BW + 8, source], BW - 1, 1)
                far = jnp.broadcast_to(far[7:8, :], (BW, BW))
                left = jnp.where(lane > own, tile, jnp.where(lane == own, far, 0.0))
                lefts[0][pl.ds(begin, BW), :] = left
                diags[0][pl.ds(begin, BW), :] = jnp.where(lane <= own, tile, 0.0)
            return carry

        lax.fori_loop(0, part.shape[0], lay_out, 0)

    def mirror(index, carry):
        places = [pl.ds(pl.multiple_of((index * 7 + i) * BW + BW, 8), BW) for i in range(7)]
        lowers = [diags[0][at, :] for at in places]
        for at, lower in zip(places, lowers):
            diags[0][at, :] = jnp.where(lane <= sub, lower, lower.T)
        return carry

    lax.fori_loop(0, (order // BW + 1) // 7, mirror, 0)

    def slot_of(window):
        index = window - first_window
        return jnp.where((index >= 0) & (index < SLOTS - 1), index, SLOTS - 1)

    def left_over(s, last):
        entries = jnp.zeros((1, BW), jnp.float32)
        for back in range(1, s + 1):
            entry = work[s - back, back : back + 1, :]
            entries = jnp.where((line == s - back) & last, entry, entries)
        return entries

    def stage(t, carry):
        for s in reversed(range(SWEEPS)):
            k = jnp.maximum(t - 2 * s, -1)
            following = t - 2 * s + 1
            base = k * BW + (s + 1 + OFF)
            here = pl.ds(base, BW)
            below = pl.ds(base + BW, BW)
            u_col = kept[s][slot_of(jnp.where(following == k + 1, k, -1000))]
            u_row = rows[s, 0:1, :]
            u_before = rows[s, 1:2, :]
            u_head = rows[s, 2:3, :]
            corner = rows[s, 3:4, :]
            b_last = rows[s, 5:6, :]

            left = lefts[s][here, :]
            low = lefts[s][below, :]
            if s > 0:
                other = rows[s - 1, 3:4, :]
                patch = jnp.where(line == s - 1, other, left_over(s - 1, k == steps - 2))
                low = with_last(low, patch)
            b = spread(lane_sum(low * u_row))
            pick = jnp.where(following == 0, (s - 1) % BW, s)
            first = lane_sum(jnp.where(line == pick, low, 0.0))
            x_col = spread(first) - b * u_head
            low = low - b * u_row
            x_row = row_sum(
                tree_sum([jnp.where(turn8 == s + 8 * i, x_col[8 * i : 8 * i + 8], 0.0) for i in range(BW // 8)])
            )
            x_head = x_col[0:1, :]
            rest_row = jnp.where(line == s, 0.0, x_row)
            rest_col = with_first(x_col, jnp.zeros((1, BW), jnp.float32))
            rest = row_sum(rest_col * rest_col)
            length = jnp.sqrt(rest + x_head * x_head)
            head = x_head + length
            size = rest + head * head
            valid = (following >= 0) & (following < steps)
            scale = jnp.where(valid, lax.rsqrt(0.5 * size), 0.0)
            next_head = jnp.where(valid, scale * head, 0.0)
            next_row = scale * rest_row + jnp.where(line == s, next_head, 0.0)
            next_col = with_first(scale * x_col, next_head)
            next_corner = jnp.where(valid, -length, x_head)

            left_last = left[BW - 1 : BW, :]
            if s > 0:
                left = with_last(left, left_last - b_last * u_before)
            a_row = row_sum(u_col * left)
            left = left - u_col * a_row
            mid = diags[s][here, :]
            y_row = row_sum(u_col * mid)
            entering, unit = None, None
            if s > 0:
                last_row = mid[BW - 1 : BW, :]
                column = line == s - 1
                y_row = jnp.where(column, lane_sum(u_row * last_row), y_row)
                mid = with_last(jnp.where(column, 0.0, mid), last_row)
                entering = jnp.where(column, 0.0, last_row)
                unit = jnp.where(column, -1.0, 0.0)
            product = lane_sum(u_row * y_row)
            change = outer_sum(u_row, y_row, entering, unit)
            if s > 0:
                turned[s, 0:BW, :] = change
                turned[s, BW : BW + 8, :] = change[0:8, :]
                change = turned[s, s : s + BW, :]
            mid = mid - u_col * (y_row - product * u_row) - change
            new_left = jnp.where(line == s, mid, left)
            new_left = with_first(new_left, jnp.where(line == s, corner, left_over(s, k == steps)))
            new_mid = with_first(mid, jnp.where(line == s, mid[0:1, :], left[0:1, :]))
            lefts[s][below, :] = low
            lefts[s + 1][here, :] = new_left
            diags[s + 1][here, :] = new_mid
            rows[s, 0:1, :] = next_row
            rows[s, 1:2, :] = u_row
            rows[s, 2:3, :] = next_head
            rows[s, 3:4, :] = next_corner
            kept[s][slot_of(following)] = next_col
            rows[s, 4:5, :] = corner
            rows[s, 5:6, :] = b[BW - 1 : BW, :]

        @pl.when((t < 2 * SWEEPS) | (t >= steps - 1))
        def _():
            for s in range(SWEEPS):
                base = jnp.maximum(t - 2 * s, -1) * BW + (s + 1 + OFF)

                @pl.when(t - 2 * s == steps - 1)
                def _():
                    low = lefts[s][pl.ds(base + BW, BW), :]
                    column = spread(lane_sum(jnp.where(line == s, low, 0.0)))
                    if s > 0:
                        head = lane_sum(jnp.where(line == s, rows[s, 1:2, :], 0.0))
                        column = with_last(column, -rows[s, 5:6, :] * head)
                    work[s] = column

                @pl.when(t == 2 * s)
                def _():
                    column = line == (s - 1) % BW
                    at = pl.ds(base, BW)
                    left = lefts[s + 1][at, :]
                    lefts[s + 1][at, :] = jnp.where(column | (sub == 0), 0.0, left)
                    top = pl.ds(base, 1)
                    diags[s + 1][top, :] = jnp.where(column, rows[s, 4:5, :], diags[s + 1][top, :])

        return carry

    lax.fori_loop(-1, steps + 2 * SWEEPS, stage, 0)

    count = band_out.shape[1]
    for block in range(count // BW):
        begin = device * count + block * BW
        low = lefts[4][pl.ds(begin + OFF, BW), :]
        mid = diags[4][pl.ds(begin + OFF, BW), :]
        row = begin + sub
        place_i = (row - (SWEEPS + 1)) & (BW - 1)
        place_j = (lane - SWEEPS) & (BW - 1)
        inner = jnp.where(place_j <= place_i, mid, low)
        outer = jnp.where(place_j <= place_i, low, 0.0)
        for s in range(SWEEPS):
            top = steps * BW + s + 1
            gap = (begin - top) & (BW - 1)
            tail = pltpu.roll(work[s], BW - gap, 0)
            inside = (row > steps * BW + SWEEPS) & (row < top + BW) & (lane == s)
            outer = jnp.where(inside, tail, outer)
        chosen = jnp.where(slice_index < SWEEPS * 2, inner, outer)
        chosen = pltpu.roll(chosen, 1, 1)
        for bit in range(7):
            step = 1 << bit
            chosen = jnp.where((sub & step) != 0, pltpu.roll(chosen, BW - step, 1), chosen)
        work[SWEEPS] = chosen.T
        for index in range(band_out.shape[0]):
            source = (-(slice_index * band_out.shape[0] + index)) & (BW - 1)
            band_out[index : index + 1, pl.ds(block * BW, BW)] = work[SWEEPS, pl.ds(source, 1), :]

    begin = 0
    for slab in slabs:
        held[begin : begin + slab.shape[0], :] = slab[...]
        begin += slab.shape[0]
    for s in reversed(range(SWEEPS)):
        for window in range(SWEEPS - 1 - s, SLOTS - 1):
            at = pl.ds(window * BW + s + 1, BW)
            block = held[at, :]
            u_col = kept[s][window]
            held[at, :] = block - u_col * row_sum(u_col * block)
    slab_out[...] = held[pl.ds(HALO, slab_out.shape[0]), :]


def run_chase(place, slabs, parts, kinds, band_shape, slab_shape):
    order = kinds[0][3]
    rows = (OFF + (order // BW + 7) * BW + 2 * BW) // 8 * 8
    vmem = pl.BlockSpec(memory_space=pltpu.VMEM)
    return pl.pallas_call(
        functools.partial(chase_kernel, kinds),
        out_shape=(
            jax.ShapeDtypeStruct(band_shape, jnp.float32),
            jax.ShapeDtypeStruct(slab_shape, jnp.float32),
        ),
        in_specs=[pl.BlockSpec(memory_space=pltpu.SMEM)] + [vmem] * (len(slabs) + len(parts)),
        out_specs=(vmem, vmem),
        scratch_shapes=[pltpu.VMEM((rows, BW), jnp.float32)] * 10
        + [
            pltpu.VMEM((SWEEPS, 8, BW), jnp.float32),
            pltpu.VMEM((SWEEPS + 1, BW, BW), jnp.float32),
            pltpu.VMEM((HALO + slab_shape[0] + TAIL, slab_shape[1]), jnp.float32),
            pltpu.VMEM((SWEEPS, BW + 8, BW), jnp.float32),
        ]
        + [pltpu.VMEM((SLOTS, BW, BW), jnp.float32)] * SWEEPS,
        compiler_params=pltpu.CompilerParams(vmem_limit_bytes=60 << 20),
    )(place, *slabs, *parts)


def body(band_diagonals, eigenvectors):
    device = lax.axis_index("band")
    column = lax.axis_index("cols")
    rows_dev, columns = eigenvectors.shape
    devices = lax.axis_size("band")
    order = rows_dev * devices
    up = lambda by: [(i, i + by) for i in range(devices) if 0 <= i + by < devices]
    above_1 = lax.ppermute(eigenvectors, "band", up(1))
    above_2 = lax.ppermute(eigenvectors[rows_dev - (HALO - rows_dev) :], "band", up(2))
    beyond = lax.ppermute(eigenvectors[:TAIL], "band", up(-1))

    peers = lax.axis_size("cols")
    count_dev, length = band_diagonals.shape
    place_in = lax.broadcasted_iota(jnp.int32, (peers * count_dev, count_dev), 0) % count_dev
    place_of = lax.broadcasted_iota(jnp.int32, (peers * count_dev, count_dev), 1)
    pick = jnp.where(place_in + place_of == count_dev - 1, 1.0, 0.0)
    copies = jnp.dot(pick, band_diagonals, precision=lax.Precision.HIGHEST)
    pieces = lax.all_to_all(copies.reshape(peers, count_dev, length), "cols", 0, 0, tiled=True)
    pieces, above_1, above_2, beyond = lax.optimization_barrier((pieces, above_1, above_2, beyond))
    slabs = (above_2, above_1, eigenvectors, beyond)
    count = BW // count_dev
    parts = [pieces[i] for i in reversed(range(count))] + [pieces[count, -8:]]
    own_part = jnp.concatenate(parts, 0)
    quarter = devices // 4
    groups = [[y * 4 + i for y in range(quarter)] for i in range(4)]
    part_y = lax.all_gather(own_part, "band", axis=0, axis_index_groups=groups)

    def swap(x, band_bits, cols_bits):
        pairs = [
            (i * peers + j, (i ^ band_bits) * peers + (j ^ cols_bits))
            for i in range(devices)
            for j in range(peers)
        ]
        return lax.ppermute(x, ("band", "cols"), pairs)

    half = quarter // 2
    part_a = swap(part_y[:half], 2, 0)
    part_b = swap(part_y[half:], 2, peers // 2)
    parts = [part_y, part_a, part_b]
    parts += [swap(part, 1, 0) for part in parts]
    kinds = [(core, side, first, order) for core in (0, 1) for side, first in ((0, 0), (1, 0), (1, half))]
    place = jnp.stack([device, column]).astype(jnp.int32)

    return run_chase(place, slabs, parts, kinds, band_diagonals.shape, eigenvectors.shape)


def solution(mesh):
    return jax.shard_map(
        body,
        mesh=mesh,
        in_specs=(P("cols", "band"), P("band", "cols")),
        out_specs=(P("cols", "band"), P("band", "cols")),
        check_vma=False,
    )
```

```python
import functools

import jax
import jax.numpy as jnp
from jax import lax
from jax.experimental import pallas as pl
from jax.experimental.pallas import tpu as pltpu
from jax.sharding import PartitionSpec as P

SWEEPS = 4
BW = 128
OFF = 255
HALO = 512
TAIL = 8
SLOTS = 8


def lane_sum(x):
    return jnp.sum(x, axis=1, keepdims=True)


def row_sum(x):
    return jnp.sum(x, axis=0, keepdims=True)


def spread(x):
    return jnp.broadcast_to(x, (x.shape[0], BW))


def with_first(x, row):
    index = lax.broadcasted_iota(jnp.int32, (8, BW), 0)
    return jnp.concatenate([jnp.where(index == 0, row, x[:8]), x[8:]], 0)


def with_last(x, row):
    index = lax.broadcasted_iota(jnp.int32, (8, BW), 0)
    return jnp.concatenate([x[:-8], jnp.where(index == 7, row, x[-8:])], 0)


def tree_sum(terms):
    while len(terms) > 1:
        terms = [sum(terms[i : i + 2][1:], terms[i]) for i in range(0, len(terms), 2)]
    return terms[0]


def in_three(x):
    high = x.astype(jnp.bfloat16).astype(jnp.float32)
    rest = x - high
    middle = rest.astype(jnp.bfloat16).astype(jnp.float32)
    return high, middle, rest - middle


def fill(index, base, values):
    for places, value in values:
        mask = index == places[0]
        for place in places[1:]:
            mask = mask | (index == place)
        base = jnp.where(mask, value, base)
    return base


def outer_sum(u, y, entering, unit):
    index = lax.broadcasted_iota(jnp.int32, (16, BW), 0)
    zero = jnp.zeros((16, BW), jnp.float32)
    u1, u2, u3 = in_three(u)
    left, right = zero, fill(index, zero, [((0, 2, 5), u1), ((1, 3), u2), ((4,), u3)])
    if entering is not None:
        e1, e2, e3 = in_three(entering)
        left = fill(index, left, [((6,), e1), ((7,), e2), ((8,), e3)])
        right = fill(index, right, [((6, 7, 8), unit)])
    y1, y2, y3 = in_three(y)
    left = fill(index, left, [((0, 1, 4), y1), ((2, 3), y2), ((5,), y3)])
    return lax.dot_general(
        left.astype(jnp.bfloat16),
        right.astype(jnp.bfloat16),
        (((0,), (0,)), ((), ())),
        preferred_element_type=jnp.float32,
    )


def chase_kernel(kinds, *refs):
    place, slabs = refs[0], refs[1:5]
    parts = refs[5 : 5 + len(kinds)]
    band_out, slab_out = refs[5 + len(kinds) : 7 + len(kinds)]
    scratch = refs[7 + len(kinds) :]
    lefts = scratch[0:5]
    diags = scratch[5:10]
    rows, work, held, turned = scratch[10:14]
    kept = scratch[14:18]
    order = kinds[0][3]
    steps = order // BW - 2
    device, slice_index = place[0], place[1]
    first_window = (device * slab_out.shape[0]) // BW - HALO // BW

    lane = lax.broadcasted_iota(jnp.int32, (BW, BW), 1)
    sub = lax.broadcasted_iota(jnp.int32, (BW, BW), 0)
    line = lax.broadcasted_iota(jnp.int32, (1, BW), 1)
    turn8 = (lane[:8] - sub[:8]) & (BW - 1)

    zero_block = jnp.zeros((BW, BW), jnp.float32)
    for ref in lefts + diags:
        for block in range(4):
            ref[pl.ds(block * BW, BW), :] = zero_block
    for ref in (lefts[0], diags[0]):
        start = (order + OFF) // 8 * 8
        ref[pl.ds(start, ref.shape[0] - start), :] = jnp.zeros((ref.shape[0] - start, BW), jnp.float32)
    for s in range(SWEEPS):
        rows[s] = jnp.zeros((8, BW), jnp.float32)
        for slot in range(SLOTS):
            kept[s][slot] = zero_block

    own = (sub - 1) & (BW - 1)

    for part, (core, side, first, _) in zip(parts, kinds):
        length = part.shape[2]

        def lay_out(index, carry):
            owner = (index + first) * 4 + ((device & 3) ^ (2 * side + core))
            for block in range(length // BW):
                source = pl.ds(block * BW, BW)
                begin = pl.multiple_of(owner * length + block * BW, BW) + OFF
                tile = part[index, 0:BW, source].T
                tile = pltpu.roll(tile, 0, 1, stride=1, stride_axis=0)
                far = pltpu.roll(part[index, BW : BW + 8, source], BW - 1, 1)
                far = jnp.broadcast_to(far[7:8, :], (BW, BW))
                left = jnp.where(lane > own, tile, jnp.where(lane == own, far, 0.0))
                lefts[0][pl.ds(begin, BW), :] = left
                diags[0][pl.ds(begin, BW), :] = jnp.where(lane <= own, tile, 0.0)
            return carry

        lax.fori_loop(0, part.shape[0], lay_out, 0)

    def mirror(index, carry):
        places = [pl.ds(pl.multiple_of((index * 7 + i) * BW + BW, 8), BW) for i in range(7)]
        lowers = [diags[0][at, :] for at in places]
        for at, lower in zip(places, lowers):
            diags[0][at, :] = jnp.where(lane <= sub, lower, lower.T)
        return carry

    lax.fori_loop(0, (order // BW + 1) // 7, mirror, 0)

    def slot_of(window):
        index = window - first_window
        return jnp.where((index >= 0) & (index < SLOTS - 1), index, SLOTS - 1)

    def left_over(s, last):
        entries = jnp.zeros((1, BW), jnp.float32)
        for back in range(1, s + 1):
            entry = work[s - back, back : back + 1, :]
            entries = jnp.where((line == s - back) & last, entry, entries)
        return entries

    def stage(t, carry):
        for s in reversed(range(SWEEPS)):
            k = jnp.maximum(t - 2 * s, -1)
            following = t - 2 * s + 1
            base = k * BW + (s + 1 + OFF)
            here = pl.ds(base, BW)
            below = pl.ds(base + BW, BW)
            u_col = kept[s][slot_of(jnp.where(following == k + 1, k, -1000))]
            u_row = rows[s, 0:1, :]
            u_before = rows[s, 1:2, :]
            u_head = rows[s, 2:3, :]
            corner = rows[s, 3:4, :]
            b_last = rows[s, 5:6, :]

            left = lefts[s][here, :]
            left_last = left[BW - 1 : BW, :]
            if s > 0:
                left = with_last(left, left_last - b_last * u_before)
            a_row = row_sum(u_col * left)
            left = left - u_col * a_row
            mid = diags[s][here, :]
            y_row = row_sum(u_col * mid)
            entering, unit = None, None
            if s > 0:
                last_row = mid[BW - 1 : BW, :]
                column = line == s - 1
                y_row = jnp.where(column, lane_sum(u_row * last_row), y_row)
                mid = with_last(jnp.where(column, 0.0, mid), last_row)
                entering = jnp.where(column, 0.0, last_row)
                unit = jnp.where(column, -1.0, 0.0)
            product = lane_sum(u_row * y_row)
            change = outer_sum(u_row, y_row, entering, unit)
            if s > 0:
                turned[s, 0:BW, :] = change
                turned[s, BW : BW + 8, :] = change[0:8, :]
                change = turned[s, s : s + BW, :]
            mid = mid - u_col * (y_row - product * u_row) - change
            low = lefts[s][below, :]
            if s > 0:
                other = rows[s - 1, 3:4, :]
                patch = jnp.where(line == s - 1, other, left_over(s - 1, k == steps - 2))
                low = with_last(low, patch)
            b = spread(lane_sum(low * u_row))
            pick = jnp.where(following == 0, (s - 1) % BW, s)
            first = lane_sum(jnp.where(line == pick, low, 0.0))
            x_col = spread(first) - b * u_head
            low = low - b * u_row
            x_row = row_sum(
                tree_sum([jnp.where(turn8 == s + 8 * i, x_col[8 * i : 8 * i + 8], 0.0) for i in range(BW // 8)])
            )
            x_head = x_col[0:1, :]
            rest_row = jnp.where(line == s, 0.0, x_row)
            rest_col = with_first(x_col, jnp.zeros((1, BW), jnp.float32))
            rest = row_sum(rest_col * rest_col)
            length = jnp.sqrt(rest + x_head * x_head)
            head = x_head + length
            size = rest + head * head
            valid = (following >= 0) & (following < steps)
            scale = jnp.where(valid, lax.rsqrt(0.5 * size), 0.0)
            next_head = jnp.where(valid, scale * head, 0.0)
            next_row = scale * rest_row + jnp.where(line == s, next_head, 0.0)
            next_col = with_first(scale * x_col, next_head)
            next_corner = jnp.where(valid, -length, x_head)
            new_left = jnp.where(line == s, mid, left)
            new_left = with_first(new_left, jnp.where(line == s, corner, left_over(s, k == steps)))
            new_mid = with_first(mid, jnp.where(line == s, mid[0:1, :], left[0:1, :]))
            lefts[s][below, :] = low
            lefts[s + 1][here, :] = new_left
            diags[s + 1][here, :] = new_mid
            rows[s, 0:1, :] = next_row
            rows[s, 1:2, :] = u_row
            rows[s, 2:3, :] = next_head
            rows[s, 3:4, :] = next_corner
            kept[s][slot_of(following)] = next_col
            rows[s, 4:5, :] = corner
            rows[s, 5:6, :] = b[BW - 1 : BW, :]

        @pl.when((t < 2 * SWEEPS) | (t >= steps - 1))
        def _():
            for s in range(SWEEPS):
                base = jnp.maximum(t - 2 * s, -1) * BW + (s + 1 + OFF)

                @pl.when(t - 2 * s == steps - 1)
                def _():
                    low = lefts[s][pl.ds(base + BW, BW), :]
                    column = spread(lane_sum(jnp.where(line == s, low, 0.0)))
                    if s > 0:
                        head = lane_sum(jnp.where(line == s, rows[s, 1:2, :], 0.0))
                        column = with_last(column, -rows[s, 5:6, :] * head)
                    work[s] = column

                @pl.when(t == 2 * s)
                def _():
                    column = line == (s - 1) % BW
                    at = pl.ds(base, BW)
                    left = lefts[s + 1][at, :]
                    lefts[s + 1][at, :] = jnp.where(column | (sub == 0), 0.0, left)
                    top = pl.ds(base, 1)
                    diags[s + 1][top, :] = jnp.where(column, rows[s, 4:5, :], diags[s + 1][top, :])

        return carry

    lax.fori_loop(-1, steps + 2 * SWEEPS, stage, 0)

    count = band_out.shape[1]
    for block in range(count // BW):
        begin = device * count + block * BW
        low = lefts[4][pl.ds(begin + OFF, BW), :]
        mid = diags[4][pl.ds(begin + OFF, BW), :]
        row = begin + sub
        place_i = (row - (SWEEPS + 1)) & (BW - 1)
        place_j = (lane - SWEEPS) & (BW - 1)
        inner = jnp.where(place_j <= place_i, mid, low)
        outer = jnp.where(place_j <= place_i, low, 0.0)
        for s in range(SWEEPS):
            top = steps * BW + s + 1
            gap = (begin - top) & (BW - 1)
            tail = pltpu.roll(work[s], BW - gap, 0)
            inside = (row > steps * BW + SWEEPS) & (row < top + BW) & (lane == s)
            outer = jnp.where(inside, tail, outer)
        chosen = jnp.where(slice_index < SWEEPS * 2, inner, outer)
        chosen = pltpu.roll(chosen, 1, 1)
        for bit in range(7):
            step = 1 << bit
            chosen = jnp.where((sub & step) != 0, pltpu.roll(chosen, BW - step, 1), chosen)
        work[SWEEPS] = chosen.T
        for index in range(band_out.shape[0]):
            source = (-(slice_index * band_out.shape[0] + index)) & (BW - 1)
            band_out[index : index + 1, pl.ds(block * BW, BW)] = work[SWEEPS, pl.ds(source, 1), :]

    begin = 0
    for slab in slabs:
        held[begin : begin + slab.shape[0], :] = slab[...]
        begin += slab.shape[0]
    for s in reversed(range(SWEEPS)):
        for window in range(SWEEPS - 1 - s, SLOTS - 1):
            at = pl.ds(window * BW + s + 1, BW)
            block = held[at, :]
            u_col = kept[s][window]
            held[at, :] = block - u_col * row_sum(u_col * block)
    slab_out[...] = held[pl.ds(HALO, slab_out.shape[0]), :]


def run_chase(place, slabs, parts, kinds, band_shape, slab_shape):
    order = kinds[0][3]
    rows = (OFF + (order // BW + 7) * BW + 2 * BW) // 8 * 8
    vmem = pl.BlockSpec(memory_space=pltpu.VMEM)
    return pl.pallas_call(
        functools.partial(chase_kernel, kinds),
        out_shape=(
            jax.ShapeDtypeStruct(band_shape, jnp.float32),
            jax.ShapeDtypeStruct(slab_shape, jnp.float32),
        ),
        in_specs=[pl.BlockSpec(memory_space=pltpu.SMEM)] + [vmem] * (len(slabs) + len(parts)),
        out_specs=(vmem, vmem),
        scratch_shapes=[pltpu.VMEM((rows, BW), jnp.float32)] * 10
        + [
            pltpu.VMEM((SWEEPS, 8, BW), jnp.float32),
            pltpu.VMEM((SWEEPS + 1, BW, BW), jnp.float32),
            pltpu.VMEM((HALO + slab_shape[0] + TAIL, slab_shape[1]), jnp.float32),
            pltpu.VMEM((SWEEPS, BW + 8, BW), jnp.float32),
        ]
        + [pltpu.VMEM((SLOTS, BW, BW), jnp.float32)] * SWEEPS,
        compiler_params=pltpu.CompilerParams(vmem_limit_bytes=60 << 20),
    )(place, *slabs, *parts)


def body(band_diagonals, eigenvectors):
    device = lax.axis_index("band")
    column = lax.axis_index("cols")
    rows_dev, columns = eigenvectors.shape
    devices = lax.axis_size("band")
    order = rows_dev * devices
    up = lambda by: [(i, i + by) for i in range(devices) if 0 <= i + by < devices]
    above_1 = lax.ppermute(eigenvectors, "band", up(1))
    above_2 = lax.ppermute(eigenvectors[rows_dev - (HALO - rows_dev) :], "band", up(2))
    beyond = lax.ppermute(eigenvectors[:TAIL], "band", up(-1))

    peers = lax.axis_size("cols")
    count_dev, length = band_diagonals.shape
    place_in = lax.broadcasted_iota(jnp.int32, (peers * count_dev, count_dev), 0) % count_dev
    place_of = lax.broadcasted_iota(jnp.int32, (peers * count_dev, count_dev), 1)
    pick = jnp.where(place_in + place_of == count_dev - 1, 1.0, 0.0)
    copies = jnp.dot(pick, band_diagonals, precision=lax.Precision.HIGHEST)
    pieces = lax.all_to_all(copies.reshape(peers, count_dev, length), "cols", 0, 0, tiled=True)
    pieces, above_1, above_2, beyond = lax.optimization_barrier((pieces, above_1, above_2, beyond))
    slabs = (above_2, above_1, eigenvectors, beyond)
    count = BW // count_dev
    parts = [pieces[i] for i in reversed(range(count))] + [pieces[count, -8:]]
    own_part = jnp.concatenate(parts, 0)
    quarter = devices // 4
    groups = [[y * 4 + i for y in range(quarter)] for i in range(4)]
    part_y = lax.all_gather(own_part, "band", axis=0, axis_index_groups=groups)

    def swap(x, band_bits, cols_bits):
        pairs = [
            (i * peers + j, (i ^ band_bits) * peers + (j ^ cols_bits))
            for i in range(devices)
            for j in range(peers)
        ]
        return lax.ppermute(x, ("band", "cols"), pairs)

    half = quarter // 2
    part_a = swap(part_y[:half], 2, 0)
    part_b = swap(part_y[half:], 2, peers // 2)
    parts = [part_y, part_a, part_b]
    parts += [swap(part, 1, 0) for part in parts]
    kinds = [(core, side, first, order) for core in (0, 1) for side, first in ((0, 0), (1, 0), (1, half))]
    place = jnp.stack([device, column]).astype(jnp.int32)

    return run_chase(place, slabs, parts, kinds, band_diagonals.shape, eigenvectors.shape)


def solution(mesh):
    return jax.shard_map(
        body,
        mesh=mesh,
        in_specs=(P("cols", "band"), P("band", "cols")),
        out_specs=(P("cols", "band"), P("band", "cols")),
        check_vma=False,
    )
```

```python
import functools

import jax
import jax.numpy as jnp
from jax import lax
from jax.experimental import pallas as pl
from jax.experimental.pallas import tpu as pltpu
from jax.sharding import PartitionSpec as P

SWEEPS = 4
BW = 128
OFF = 255
HALO = 512
TAIL = 8
SLOTS = 8


def lane_sum(x):
    return jnp.sum(x, axis=1, keepdims=True)


def row_sum(x):
    return jnp.sum(x, axis=0, keepdims=True)


def spread(x):
    return jnp.broadcast_to(x, (x.shape[0], BW))


def with_first(x, row):
    index = lax.broadcasted_iota(jnp.int32, (8, BW), 0)
    return jnp.concatenate([jnp.where(index == 0, row, x[:8]), x[8:]], 0)


def with_last(x, row):
    index = lax.broadcasted_iota(jnp.int32, (8, BW), 0)
    return jnp.concatenate([x[:-8], jnp.where(index == 7, row, x[-8:])], 0)


def tree_sum(terms):
    while len(terms) > 1:
        terms = [sum(terms[i : i + 2][1:], terms[i]) for i in range(0, len(terms), 2)]
    return terms[0]


def in_three(x):
    high = x.astype(jnp.bfloat16).astype(jnp.float32)
    rest = x - high
    middle = rest.astype(jnp.bfloat16).astype(jnp.float32)
    return high, middle, rest - middle


def fill(index, base, values):
    for places, value in values:
        mask = index == places[0]
        for place in places[1:]:
            mask = mask | (index == place)
        base = jnp.where(mask, value, base)
    return base


def outer_sum(u, y, entering, unit):
    index = lax.broadcasted_iota(jnp.int32, (16, BW), 0)
    zero = jnp.zeros((16, BW), jnp.float32)
    u1, u2, u3 = in_three(u)
    left, right = zero, fill(index, zero, [((0, 2, 5), u1), ((1, 3), u2), ((4,), u3)])
    if entering is not None:
        e1, e2, e3 = in_three(entering)
        left = fill(index, left, [((6,), e1), ((7,), e2), ((8,), e3)])
        right = fill(index, right, [((6, 7, 8), unit)])
    y1, y2, y3 = in_three(y)
    left = fill(index, left, [((0, 1, 4), y1), ((2, 3), y2), ((5,), y3)])
    return lax.dot_general(
        left.astype(jnp.bfloat16),
        right.astype(jnp.bfloat16),
        (((0,), (0,)), ((), ())),
        preferred_element_type=jnp.float32,
    )


def chase_kernel(kinds, *refs):
    place, slabs = refs[0], refs[1:5]
    parts = refs[5 : 5 + len(kinds)]
    band_out, slab_out = refs[5 + len(kinds) : 7 + len(kinds)]
    scratch = refs[7 + len(kinds) :]
    lefts = scratch[0:5]
    diags = scratch[5:10]
    rows, work, held, turned = scratch[10:14]
    kept = scratch[14:18]
    order = kinds[0][3]
    steps = order // BW - 2
    device, slice_index = place[0], place[1]
    first_window = (device * slab_out.shape[0]) // BW - HALO // BW

    lane = lax.broadcasted_iota(jnp.int32, (BW, BW), 1)
    sub = lax.broadcasted_iota(jnp.int32, (BW, BW), 0)
    line = lax.broadcasted_iota(jnp.int32, (1, BW), 1)
    turn8 = (lane[:8] - sub[:8]) & (BW - 1)

    zero_block = jnp.zeros((BW, BW), jnp.float32)
    for ref in lefts + diags:
        for block in range(4):
            ref[pl.ds(block * BW, BW), :] = zero_block
    for ref in (lefts[0], diags[0]):
        start = (order + OFF) // 8 * 8
        ref[pl.ds(start, ref.shape[0] - start), :] = jnp.zeros((ref.shape[0] - start, BW), jnp.float32)
    for s in range(SWEEPS):
        rows[s] = jnp.zeros((8, BW), jnp.float32)
        for slot in (0, 1, 2, 3, SLOTS - 1):
            kept[s][slot] = zero_block

    own = (sub - 1) & (BW - 1)

    for part, (core, side, first, _) in zip(parts, kinds):
        length = part.shape[2]

        def lay_out(pair, carry):
            for index in (2 * pair, 2 * pair + 1):
                owner = (index + first) * 4 + ((device & 3) ^ (2 * side + core))
                for block in range(length // BW):
                    source = pl.ds(block * BW, BW)
                    begin = pl.multiple_of(owner * length + block * BW, BW) + OFF
                    tile = part[index, 0:BW, source].T
                    tile = pltpu.roll(tile, 0, 1, stride=1, stride_axis=0)
                    far = pltpu.roll(part[index, BW : BW + 8, source], BW - 1, 1)
                    far = jnp.broadcast_to(far[7:8, :], (BW, BW))
                    left = jnp.where(lane > own, tile, jnp.where(lane == own, far, 0.0))
                    lefts[0][pl.ds(begin, BW), :] = left
                    diags[0][pl.ds(begin, BW), :] = jnp.where(lane <= own, tile, 0.0)
            return carry

        lax.fori_loop(0, part.shape[0] // 2, lay_out, 0)

    def mirror(index, carry):
        places = [pl.ds(pl.multiple_of((index * 7 + i) * BW + BW, 8), BW) for i in range(7)]
        lowers = [diags[0][at, :] for at in places]
        for at, lower in zip(places, lowers):
            diags[0][at, :] = jnp.where(lane <= sub, lower, lower.T)
        return carry

    lax.fori_loop(0, (order // BW + 1) // 7, mirror, 0)

    def slot_of(window):
        index = window - first_window
        return jnp.where((index >= 0) & (index < SLOTS - 1), index, SLOTS - 1)

    def left_over(s, last):
        entries = jnp.zeros((1, BW), jnp.float32)
        for back in range(1, s + 1):
            entry = work[s - back, back : back + 1, :]
            entries = jnp.where((line == s - back) & last, entry, entries)
        return entries

    def stage(t, carry):
        for s in reversed(range(SWEEPS)):
            k = jnp.maximum(t - 2 * s, -1)
            following = t - 2 * s + 1
            base = k * BW + (s + 1 + OFF)
            here = pl.ds(base, BW)
            below = pl.ds(base + BW, BW)
            u_col = kept[s][slot_of(jnp.where(following == k + 1, k, -1000))]
            u_row = rows[s, 0:1, :]
            u_before = rows[s, 1:2, :]
            u_head = rows[s, 2:3, :]
            corner = rows[s, 3:4, :]
            b_last = rows[s, 5:6, :]

            left = lefts[s][here, :]
            left_last = left[BW - 1 : BW, :]
            if s > 0:
                left = with_last(left, left_last - b_last * u_before)
            a_row = row_sum(u_col * left)
            left = left - u_col * a_row
            mid = diags[s][here, :]
            y_row = row_sum(u_col * mid)
            entering, unit = None, None
            if s > 0:
                last_row = mid[BW - 1 : BW, :]
                column = line == s - 1
                y_row = jnp.where(column, lane_sum(u_row * last_row), y_row)
                mid = with_last(jnp.where(column, 0.0, mid), last_row)
                entering = jnp.where(column, 0.0, last_row)
                unit = jnp.where(column, -1.0, 0.0)
            product = lane_sum(u_row * y_row)
            change = outer_sum(u_row, y_row, entering, unit)
            if s > 0:
                turned[s, 0:BW, :] = change
                turned[s, BW : BW + 8, :] = change[0:8, :]
                change = turned[s, s : s + BW, :]
            mid = mid - u_col * (y_row - product * u_row) - change
            low = lefts[s][below, :]
            if s > 0:
                other = rows[s - 1, 3:4, :]
                patch = jnp.where(line == s - 1, other, left_over(s - 1, k == steps - 2))
                low = with_last(low, patch)
            b = spread(lane_sum(low * u_row))
            pick = jnp.where(following == 0, (s - 1) % BW, s)
            first = lane_sum(jnp.where(line == pick, low, 0.0))
            x_col = spread(first) - b * u_head
            low = low - b * u_row
            x_row = row_sum(
                tree_sum([jnp.where(turn8 == s + 8 * i, x_col[8 * i : 8 * i + 8], 0.0) for i in range(BW // 8)])
            )
            x_head = x_col[0:1, :]
            rest_row = jnp.where(line == s, 0.0, x_row)
            rest_col = with_first(x_col, jnp.zeros((1, BW), jnp.float32))
            rest = row_sum(rest_col * rest_col)
            length = jnp.sqrt(rest + x_head * x_head)
            head = x_head + length
            size = rest + head * head
            valid = (following >= 0) & (following < steps)
            scale = jnp.where(valid, lax.rsqrt(0.5 * size), 0.0)
            next_head = jnp.where(valid, scale * head, 0.0)
            next_row = scale * rest_row + jnp.where(line == s, next_head, 0.0)
            next_col = with_first(scale * x_col, next_head)
            next_corner = jnp.where(valid, -length, x_head)
            new_left = jnp.where(line == s, mid, left)
            new_left = with_first(new_left, jnp.where(line == s, corner, left_over(s, k == steps)))
            new_mid = with_first(mid, jnp.where(line == s, mid[0:1, :], left[0:1, :]))
            lefts[s][below, :] = low
            lefts[s + 1][here, :] = new_left
            diags[s + 1][here, :] = new_mid
            rows[s, 0:1, :] = next_row
            rows[s, 1:2, :] = u_row
            rows[s, 2:3, :] = next_head
            rows[s, 3:4, :] = next_corner
            kept[s][slot_of(following)] = next_col
            rows[s, 4:5, :] = corner
            rows[s, 5:6, :] = b[BW - 1 : BW, :]

        @pl.when((t < 2 * SWEEPS) | (t >= steps - 1))
        def _():
            for s in range(SWEEPS):
                base = jnp.maximum(t - 2 * s, -1) * BW + (s + 1 + OFF)

                @pl.when(t - 2 * s == steps - 1)
                def _():
                    low = lefts[s][pl.ds(base + BW, BW), :]
                    column = spread(lane_sum(jnp.where(line == s, low, 0.0)))
                    if s > 0:
                        head = lane_sum(jnp.where(line == s, rows[s, 1:2, :], 0.0))
                        column = with_last(column, -rows[s, 5:6, :] * head)
                    work[s] = column

                @pl.when(t == 2 * s)
                def _():
                    column = line == (s - 1) % BW
                    at = pl.ds(base, BW)
                    left = lefts[s + 1][at, :]
                    lefts[s + 1][at, :] = jnp.where(column | (sub == 0), 0.0, left)
                    top = pl.ds(base, 1)
                    diags[s + 1][top, :] = jnp.where(column, rows[s, 4:5, :], diags[s + 1][top, :])

        return carry

    lax.fori_loop(-1, steps + 2 * SWEEPS, stage, 0)

    count = band_out.shape[1]
    for block in range(count // BW):
        begin = device * count + block * BW
        low = lefts[4][pl.ds(begin + OFF, BW), :]
        mid = diags[4][pl.ds(begin + OFF, BW), :]
        row = begin + sub
        place_i = (row - (SWEEPS + 1)) & (BW - 1)
        place_j = (lane - SWEEPS) & (BW - 1)
        inner = jnp.where(place_j <= place_i, mid, low)
        outer = jnp.where(place_j <= place_i, low, 0.0)
        for s in range(SWEEPS):
            top = steps * BW + s + 1
            gap = (begin - top) & (BW - 1)
            tail = pltpu.roll(work[s], BW - gap, 0)
            inside = (row > steps * BW + SWEEPS) & (row < top + BW) & (lane == s)
            outer = jnp.where(inside, tail, outer)
        chosen = jnp.where(slice_index < SWEEPS * 2, inner, outer)
        chosen = pltpu.roll(chosen, 1, 1)
        for bit in range(7):
            step = 1 << bit
            chosen = jnp.where((sub & step) != 0, pltpu.roll(chosen, BW - step, 1), chosen)
        work[SWEEPS] = chosen.T
        for index in range(band_out.shape[0]):
            source = (-(slice_index * band_out.shape[0] + index)) & (BW - 1)
            band_out[index : index + 1, pl.ds(block * BW, BW)] = work[SWEEPS, pl.ds(source, 1), :]

    begin = 0
    for slab in slabs:
        held[begin : begin + slab.shape[0], :] = slab[...]
        begin += slab.shape[0]
    for s in reversed(range(SWEEPS)):
        for window in range(SWEEPS - 1 - s, SLOTS - 1):
            at = pl.ds(window * BW + s + 1, BW)
            block = held[at, :]
            u_col = kept[s][window]
            held[at, :] = block - u_col * row_sum(u_col * block)
    slab_out[...] = held[pl.ds(HALO, slab_out.shape[0]), :]


def run_chase(place, slabs, parts, kinds, band_shape, slab_shape):
    order = kinds[0][3]
    rows = (OFF + (order // BW + 7) * BW + 2 * BW) // 8 * 8
    vmem = pl.BlockSpec(memory_space=pltpu.VMEM)
    return pl.pallas_call(
        functools.partial(chase_kernel, kinds),
        out_shape=(
            jax.ShapeDtypeStruct(band_shape, jnp.float32),
            jax.ShapeDtypeStruct(slab_shape, jnp.float32),
        ),
        in_specs=[pl.BlockSpec(memory_space=pltpu.SMEM)] + [vmem] * (len(slabs) + len(parts)),
        out_specs=(vmem, vmem),
        scratch_shapes=[pltpu.VMEM((rows, BW), jnp.float32)] * 10
        + [
            pltpu.VMEM((SWEEPS, 8, BW), jnp.float32),
            pltpu.VMEM((SWEEPS + 1, BW, BW), jnp.float32),
            pltpu.VMEM((HALO + slab_shape[0] + TAIL, slab_shape[1]), jnp.float32),
            pltpu.VMEM((SWEEPS, BW + 8, BW), jnp.float32),
        ]
        + [pltpu.VMEM((SLOTS, BW, BW), jnp.float32)] * SWEEPS,
        compiler_params=pltpu.CompilerParams(vmem_limit_bytes=60 << 20),
    )(place, *slabs, *parts)


def body(band_diagonals, eigenvectors):
    device = lax.axis_index("band")
    column = lax.axis_index("cols")
    rows_dev, columns = eigenvectors.shape
    devices = lax.axis_size("band")
    order = rows_dev * devices
    up = lambda by: [(i, i + by) for i in range(devices) if 0 <= i + by < devices]
    above_1 = lax.ppermute(eigenvectors, "band", up(1))
    above_2 = lax.ppermute(eigenvectors[rows_dev - (HALO - rows_dev) :], "band", up(2))
    beyond = lax.ppermute(eigenvectors[:TAIL], "band", up(-1))

    peers = lax.axis_size("cols")
    count_dev, length = band_diagonals.shape
    place_in = lax.broadcasted_iota(jnp.int32, (peers * count_dev, count_dev), 0) % count_dev
    place_of = lax.broadcasted_iota(jnp.int32, (peers * count_dev, count_dev), 1)
    pick = jnp.where(place_in + place_of == count_dev - 1, 1.0, 0.0)
    copies = jnp.dot(pick, band_diagonals, precision=lax.Precision.HIGHEST)
    pieces = lax.all_to_all(copies.reshape(peers, count_dev, length), "cols", 0, 0, tiled=True)
    pieces, above_1, above_2, beyond = lax.optimization_barrier((pieces, above_1, above_2, beyond))
    slabs = (above_2, above_1, eigenvectors, beyond)
    count = BW // count_dev
    parts = [pieces[i] for i in reversed(range(count))] + [pieces[count, -8:]]
    own_part = jnp.concatenate(parts, 0)
    quarter = devices // 4
    groups = [[y * 4 + i for y in range(quarter)] for i in range(4)]
    part_y = lax.all_gather(own_part, "band", axis=0, axis_index_groups=groups)

    def swap(x, band_bits, cols_bits):
        pairs = [
            (i * peers + j, (i ^ band_bits) * peers + (j ^ cols_bits))
            for i in range(devices)
            for j in range(peers)
        ]
        return lax.ppermute(x, ("band", "cols"), pairs)

    half = quarter // 2
    part_a = swap(part_y[:half], 2, 0)
    part_b = swap(part_y[half:], 2, peers // 2)
    parts = [part_y, part_a, part_b]
    parts += [swap(part, 1, 0) for part in parts]
    kinds = [(core, side, first, order) for core in (0, 1) for side, first in ((0, 0), (1, 0), (1, half))]
    place = jnp.stack([device, column]).astype(jnp.int32)

    return run_chase(place, slabs, parts, kinds, band_diagonals.shape, eigenvectors.shape)


def solution(mesh):
    return jax.shard_map(
        body,
        mesh=mesh,
        in_specs=(P("cols", "band"), P("band", "cols")),
        out_specs=(P("cols", "band"), P("band", "cols")),
        check_vma=False,
    )
```
